32 devices in a mesh: row: 8 (over z, y), col: 4 (over x, core).
Axes of the slice: x: 2, y: 2, z: 4, core: 2. Of those that a mesh axis runs over, the one named last changes fastest.
Arguments:
- amplitude: float32 [128, 256, 256], P(('row', 'col')), may hold values from 0.1 to 3
- patches: float32 [128, 2, 256, 256], P(('row', 'col')), may hold values from -5 to 5
- dual: float32 [128, 3, 2, 256, 256], P(('row', 'col')), may hold values from -3 to 3
- probe: float32 [3, 2, 256, 256], replicated, may hold values from -6 to 6
- obj: float32 [2, 6144, 3072], P(None, 'row', 'col'), may hold values from -5 to 5
- positions: int32 [128, 2], P(('row', 'col')), may hold values from 0 to 5888, as said below
Outputs:
- dual_new: float32 [128, 3, 2, 256, 256], P(('row', 'col'))
- object_new: float32 [2, 6144, 3072], P(None, 'row', 'col')
- probe_new: float32 [3, 2, 256, 256], replicated
- patches_new: float32 [128, 2, 256, 256], P(('row', 'col'))
The draws below stay inside these ranges and needn't reach their ends.
Inputs may be any that keep to these rules, and one draw needn't show every extreme that they name: `positions`: both entries of each row are multiples of 128. A frame held by the device at index i of row and j of col has its row offset between i * 768 and (i + 1) * 768 - 128 and its column offset between j * 768 and (j + 1) * 768 - 128; every frame lies inside the object.
All inputs are finite; a program needn't handle non-finite values.
Results may differ from the reference program's by a relative error of at most 0.0003.
Values sent between devices are 32-bit elements; how exact they have to be, the bound alone decides.
No kernel may reach another device: no remote copies, remote signals or barrier semaphores. Data moves between devices by JAX's collectives and lax.ppermute only.
A program may use at most 192 MiB of HBM per device.

```python
import math
import jax
import jax.numpy as jnp
from jax import lax

FRAME = 256
MODES = 3
FR_DEV = 4
TILE = 768
SWEEPS = 4
FRAMES = 128
OBJ_ROWS = 6144
OBJ_COLS = 3072


def draw_positions(key, part):
    frame_ids = jnp.arange(FRAMES, dtype=jnp.int32)
    device_ids = frame_ids // FR_DEV
    tile_cols = OBJ_COLS // TILE
    tile_rows = OBJ_ROWS // TILE
    grid_row = device_ids // tile_cols
    grid_col = device_ids % tile_cols
    step_size = FRAME // 2
    places = TILE // step_size
    top_row = jnp.where(grid_row == tile_rows - 1, places - 1, places)
    top_col = jnp.where(grid_col == tile_cols - 1, places - 1, places)
    key_rows = jax.random.fold_in(key, 11)
    key_cols = jax.random.fold_in(key, 23)
    offset_row = jax.random.randint(key_rows, (FRAMES,), 0, top_row, dtype=jnp.int32)
    offset_col = jax.random.randint(key_cols, (FRAMES,), 0, top_col, dtype=jnp.int32)
    first = grid_row * TILE + offset_row * step_size
    second = grid_col * TILE + offset_col * step_size
    return jnp.stack([first, second], axis=1).astype(jnp.int32)


def steps_of(stream_key, dims, pieces, least, largest):
    factor_of = 1.0
    for position, parts in pieces:
        heights = jax.random.uniform(jax.random.fold_in(jax.random.fold_in(stream_key, 6), position), (parts,), jnp.float32, least / len(pieces), largest / len(pieces))
        factor_of = factor_of * jnp.repeat(jnp.exp(heights), dims[position] // parts).reshape((-1,) + (1,) * (len(dims) - 1 - position))
    return factor_of


def gaussian(rng, extent, scale, most, cuts=(), kind=jnp.bfloat16):
    entries = jax.random.normal(rng, extent, jnp.float32) * scale
    if len(cuts) > 0:
        entries = steps_of(rng, extent, cuts, -0.22, 0.18) * entries
    return jnp.clip(entries, min=-most, max=most).astype(kind)


def setup_inputs(seed: int = 0) -> dict:
    streams_of = jax.random.split(jax.random.key(seed), 7)
    return {
        "amplitude": jnp.clip(jnp.exp(math.log(3.0) - 3.4011974 * jax.random.uniform(streams_of[0], (FRAMES, FRAME, FRAME), jnp.float32) ** steps_of(streams_of[0], (FRAMES, FRAME, FRAME), ((0, 32),), -0.2, 0.2)), 0.1, 3.0),
        "patches": gaussian(streams_of[1], (FRAMES, 2, FRAME, FRAME), 0.7, 5.0, ((0, 32),), jnp.float32),
        "dual": gaussian(streams_of[2], (FRAMES, MODES, 2, FRAME, FRAME), 0.3, 3.0, ((0, 32),), jnp.float32),
        "probe": gaussian(streams_of[3], (MODES, 2, FRAME, FRAME), 1.0, 6.0, (), jnp.float32),
        "obj": gaussian(streams_of[4], (2, OBJ_ROWS, OBJ_COLS), 0.7, 5.0, ((1, 8), (2, 4)), jnp.float32),
        "positions": draw_positions(jax.random.fold_in(streams_of[6], 71), 0),
    }


amp_floor = 1.0
obj_weight = 0.5
smooth_weight = 16.0
probe_weight = 1.0

def tables(width):
    index = jnp.arange(width, dtype=jnp.int32)
    product = index[:, None] * index[None, :] % width
    angle = product.astype(jnp.float32) * (2.0 * math.pi / width)
    scaling = 1.0 / math.sqrt(width)
    return (jnp.cos(angle) * scaling, jnp.sin(angle) * scaling)

def dft_pair(real_part, imag_part, cos_tab, sin_tab):
    highest = lax.Precision.HIGHEST
    left_re = jnp.matmul(cos_tab, real_part, precision=highest) - jnp.matmul(sin_tab, imag_part, precision=highest)
    left_im = jnp.matmul(cos_tab, imag_part, precision=highest) + jnp.matmul(sin_tab, real_part, precision=highest)
    out_re = jnp.matmul(left_re, cos_tab, precision=highest) - jnp.matmul(left_im, sin_tab, precision=highest)
    out_im = jnp.matmul(left_re, sin_tab, precision=highest) + jnp.matmul(left_im, cos_tab, precision=highest)
    return (out_re, out_im)

def frame_update(amplitude, patches, dual, probe, cos_tab, sin_tab):
    patch_re = patches[:, 0][:, None]
    patch_im = patches[:, 1][:, None]
    probe_re = probe[:, 0]
    probe_im = probe[:, 1]
    exit_re = probe_re * patch_re - probe_im * patch_im
    exit_im = probe_re * patch_im + probe_im * patch_re
    dual_re = dual[:, :, 0]
    dual_im = dual[:, :, 1]
    far_re, far_im = dft_pair(exit_re + dual_re, exit_im + dual_im, cos_tab, -sin_tab)
    intensity = lax.optimization_barrier(jnp.sum(far_re * far_re + far_im * far_im, axis=1))
    ratio = (amplitude / jnp.sqrt(intensity + amp_floor))[:, None]
    near_re, near_im = dft_pair(far_re * ratio, far_im * ratio, cos_tab, sin_tab)
    new_re = dual_re + exit_re - near_re
    new_im = dual_im + exit_im - near_im
    return (new_re, new_im, near_re - new_re, near_im - new_im)

def reference(amplitude, patches, dual, probe, obj, positions):
    cos_tab, sin_tab = tables(FRAME)
    probe_re = probe[:, 0]
    probe_im = probe[:, 1]
    probe_power = lax.optimization_barrier(jnp.sum(probe_re * probe_re + probe_im * probe_im, axis=0))

    def advance(carry, item):
        canvas, probe_num, probe_den = carry
        amp_one, patch_one, dual_one, place = item
        new_re, new_im, target_re, target_im = frame_update(amp_one[None], patch_one[None], dual_one[None], probe, cos_tab, sin_tab)
        new_re, new_im, target_re, target_im = (new_re[0], new_im[0], target_re[0], target_im[0])
        patch_re = patch_one[0]
        patch_im = patch_one[1]
        probe_num = probe_num + jnp.stack([patch_re * target_re + patch_im * target_im, patch_re * target_im - patch_im * target_re], axis=1)
        probe_den = probe_den + patch_re * patch_re + patch_im * patch_im
        obj_re = lax.optimization_barrier(jnp.sum(probe_re * target_re + probe_im * target_im, axis=0))
        obj_im = lax.optimization_barrier(jnp.sum(probe_re * target_im - probe_im * target_re, axis=0))
        contrib = jnp.stack([obj_re, obj_im, probe_power])
        start = (jnp.zeros((), jnp.int32), place[0].astype(jnp.int32), place[1].astype(jnp.int32))
        current = lax.dynamic_slice(canvas, start, (3, FRAME, FRAME))
        canvas = lax.dynamic_update_slice(canvas, current + contrib, start)
        return ((canvas, probe_num, probe_den), jnp.stack([new_re, new_im], axis=1))
    init = (jnp.zeros((3, OBJ_ROWS, OBJ_COLS), jnp.float32), jnp.zeros((MODES, 2, FRAME, FRAME), jnp.float32), jnp.zeros((FRAME, FRAME), jnp.float32))
    (canvas, probe_num, probe_den), dual_new = lax.scan(advance, init, (amplitude, patches, dual, positions))
    probe_new = (probe_num + probe_weight * probe) / (probe_den + probe_weight)
    rhs = canvas[:2] + obj_weight * obj
    diagonal = canvas[2] + obj_weight + 4.0 * smooth_weight
    field = obj
    for sweep in range(SWEEPS):
        padded = jnp.pad(field, ((0, 0), (1, 1), (1, 1)))
        beside = padded[:, 2:, 1:-1] + padded[:, :-2, 1:-1] + padded[:, 1:-1, 2:] + padded[:, 1:-1, :-2]
        field = (rhs + smooth_weight * beside) / diagonal

    def window(place):
        start = (jnp.zeros((), jnp.int32), place[0].astype(jnp.int32), place[1].astype(jnp.int32))
        return lax.dynamic_slice(field, start, (2, FRAME, FRAME))
    patches_new = lax.map(window, positions)
    return (dual_new, field, probe_new, patches_new)
```

```python
import functools
import math

import jax
import jax.numpy as jnp
import numpy as np
from jax import lax
from jax.experimental import pallas as pl
from jax.experimental.pallas import tpu as pltpu
from jax.sharding import PartitionSpec as P

SWEEPS = 4
HALO = 8

amp_floor = 1.0
obj_weight = 0.5
smooth_weight = 16.0
probe_weight = 1.0

VMEM_SPEC = pl.BlockSpec(memory_space=pltpu.VMEM)
VMEM_LIMIT = 60 * 1024 * 1024


def shift(block, axis, distance):
    count = lax.axis_size(axis)
    route = [(i, i + distance) for i in range(count) if 0 <= i + distance < count]
    return lax.ppermute(block, axis, route)


def split_two(value):
    high = value.astype(jnp.bfloat16)
    low = (value - high.astype(jnp.float32)).astype(jnp.bfloat16)
    return high, low


def dft_weights(width):
    half = width // 2
    k = np.arange(half)[:, None]
    j = np.arange(half)[None, :]
    mats = []
    for parity in range(2):
        angle = 2.0 * math.pi * ((k * (2 * j + parity)) % width) / width
        re = np.cos(angle) / math.sqrt(width)
        im = -np.sin(angle) / math.sqrt(width)
        mats.append(np.block([[re, im], [-im, re]]))
    mats = mats + [m.T for m in mats]
    right, left = [], []
    for m in mats:
        high = m.astype(np.float32).astype(jnp.bfloat16)
        low = (m - high.astype(np.float64)).astype(np.float32).astype(jnp.bfloat16)
        right.append(np.concatenate([high, high, low], axis=0))
        left.append(np.concatenate([high, low, high], axis=1))
    order = np.concatenate([np.arange(0, width, 2), np.arange(1, width, 2)])
    perm = np.zeros((width, width), np.float32)
    perm[order, np.arange(width)] = 1.0
    right = np.stack(right)
    left = np.stack([left[2], left[3], left[0], left[1]])
    return right, left, perm.astype(jnp.bfloat16)


def frames_kernel(
    place_ref, amp_low_ref, amp_high_ref, patch_ref, dual_ref, probe_ref, right_ref, left_ref, perm_ref,
    new_ref, num_ref, canvas_ref, even_ref, odd_ref,
):
    frame = pl.program_id(0)
    modes = probe_ref.shape[0]
    width = probe_ref.shape[-1]
    half = width // 2

    @pl.when(frame == 0)
    def _():
        canvas_ref[...] = jnp.zeros_like(canvas_ref)
        num_ref[...] = jnp.zeros_like(num_ref)

    def dot(a, b):
        return jnp.dot(a, b, preferred_element_type=jnp.float32)

    def times_right(value, which):
        high, low = split_two(value)
        return dot(jnp.concatenate([high, low, high], axis=1), right_ref[which])

    def times_left(which, value):
        high, low = split_two(value)
        return dot(left_ref[which], jnp.concatenate([high, high, low], axis=0))

    patch_re = patch_ref[0, 0]
    patch_im = patch_ref[0, 1]

    def exit_wave(m):
        probe_re = probe_ref[m, 0]
        probe_im = probe_ref[m, 1]
        return probe_re * patch_re - probe_im * patch_im, probe_re * patch_im + probe_im * patch_re

    amps = []
    for parity in range(2):
        every = pl.ds(parity, half, stride=2)
        rows = jnp.concatenate([amp_low_ref[0, every, :], amp_high_ref[0, every, :]], axis=1)
        first = rows.astype(jnp.bfloat16)
        rest = rows - first.astype(jnp.float32)
        second, third = split_two(rest)
        amps.append(dot(first, perm_ref[...]) + (dot(second, perm_ref[...]) + dot(third, perm_ref[...])))

    power = [None, None]
    for m in range(modes):
        exit_re, exit_im = exit_wave(m)
        wave_re = exit_re + dual_ref[0, m, 0]
        wave_im = exit_im + dual_ref[0, m, 1]
        sums = jnp.concatenate(
            [wave_re[:, :half] + wave_re[:, half:], wave_im[:, :half] + wave_im[:, half:]], axis=1
        )
        diffs = jnp.concatenate(
            [wave_re[:, :half] - wave_re[:, half:], wave_im[:, :half] - wave_im[:, half:]], axis=1
        )
        even = times_right(sums, 0)
        odd = times_right(diffs, 1)

        def stack(op):
            return jnp.concatenate(
                [
                    jnp.concatenate([op(x[:half, part], x[half:, part]) for x in (even, odd)], axis=1)
                    for part in (slice(0, half), slice(half, width))
                ],
                axis=0,
            )

        far_even = times_left(0, stack(lambda a, b: a + b))
        far_odd = times_left(1, stack(lambda a, b: a - b))
        even_ref[m] = far_even
        odd_ref[m] = far_odd
        for parity, far in enumerate((far_even, far_odd)):
            term = far[:half] * far[:half] + far[half:] * far[half:]
            power[parity] = term if m == 0 else power[parity] + term

    ratios = []
    for parity in range(2):
        ratio = amps[parity] / jnp.sqrt(power[parity] + amp_floor)
        ratios.append(jnp.concatenate([ratio, ratio], axis=0))

    start_row = pl.multiple_of(place_ref[frame, 0], half)
    start_col = pl.multiple_of(place_ref[frame, 1], half)
    obj_re = jnp.zeros((width, width), jnp.float32)
    obj_im = jnp.zeros((width, width), jnp.float32)
    for m in range(modes):
        even = times_left(2, even_ref[m] * ratios[0])
        odd = times_left(3, odd_ref[m] * ratios[1])
        top = even + odd
        bottom = even - odd

        def rows_of(part):
            return jnp.concatenate(
                [
                    jnp.concatenate([x[:half, part], x[half:, part]], axis=1)
                    for x in (top, bottom)
                ],
                axis=0,
            )

        even = times_right(rows_of(slice(0, half)), 2)
        odd = times_right(rows_of(slice(half, width)), 3)
        low = even + odd
        high = even - odd
        near_re = jnp.concatenate([low[:, :half], high[:, :half]], axis=1)
        near_im = jnp.concatenate([low[:, half:], high[:, half:]], axis=1)
        exit_re, exit_im = exit_wave(m)
        new_re = dual_ref[0, m, 0] + exit_re - near_re
        new_im = dual_ref[0, m, 1] + exit_im - near_im
        new_ref[0, m, 0] = new_re
        new_ref[0, m, 1] = new_im
        target_re = near_re - new_re
        target_im = near_im - new_im
        num_ref[2 * m] += patch_re * target_re + patch_im * target_im
        num_ref[2 * m + 1] += patch_re * target_im - patch_im * target_re
        probe_re = probe_ref[m, 0]
        probe_im = probe_ref[m, 1]
        obj_re += probe_re * target_re + probe_im * target_im
        obj_im += probe_re * target_im - probe_im * target_re
    num_ref[2 * modes] += patch_re * patch_re + patch_im * patch_im
    canvas_ref[0, pl.ds(start_row, width), pl.ds(start_col, width)] += obj_re
    canvas_ref[1, pl.ds(start_row, width), pl.ds(start_col, width)] += obj_im


def frames_update(amplitude, patches, dual, probe, places, tile):
    count, modes = dual.shape[:2]
    width = amplitude.shape[-1]
    right, left, perm = dft_weights(width)
    grow = tile + width // 2

    def whole(shape):
        return pl.BlockSpec(shape, lambda f, *_: (0,) * len(shape))

    return pl.pallas_call(
        frames_kernel,
        out_shape=(
            jax.ShapeDtypeStruct(dual.shape, jnp.float32),
            jax.ShapeDtypeStruct((2 * modes + 1, width, width), jnp.float32),
            jax.ShapeDtypeStruct((2, grow, grow), jnp.float32),
        ),
        grid_spec=pltpu.PrefetchScalarGridSpec(
            num_scalar_prefetch=1,
            grid=(count,),
            in_specs=[
                pl.BlockSpec((1, width, width // 2), lambda f, *_: (f, 0, 0)),
                pl.BlockSpec((1, width, width // 2), lambda f, *_: (f, 0, 1)),
                pl.BlockSpec((1, 2, width, width), lambda f, *_: (f, 0, 0, 0)),
                pl.BlockSpec((1, modes, 2, width, width), lambda f, *_: (f, 0, 0, 0, 0)),
                whole(probe.shape),
                whole(right.shape),
                whole(left.shape),
                whole(perm.shape),
            ],
            out_specs=[
                pl.BlockSpec((1, modes, 2, width, width), lambda f, *_: (f, 0, 0, 0, 0)),
                whole((2 * modes + 1, width, width)),
                whole((2, grow, grow)),
            ],
            scratch_shapes=[
                pltpu.VMEM((modes, width, width), jnp.float32),
                pltpu.VMEM((modes, width, width), jnp.float32),
            ],
        ),
        compiler_params=pltpu.CompilerParams(vmem_limit_bytes=VMEM_LIMIT),
        cost_estimate=pl.CostEstimate(
            flops=count * modes * 24 * 2 * width**3, bytes_accessed=20 << 20, transcendentals=0
        ),
        name="frames",
    )(places, amplitude, amplitude, patches, dual, probe, jnp.asarray(right), jnp.asarray(left), jnp.asarray(perm))


def lane_of(shape):
    return lax.broadcasted_iota(jnp.int32, shape, len(shape) - 1)


def edge_block(right_part, left_part):
    lane = lane_of(right_part.shape)
    width = right_part.shape[-1]
    return jnp.where(lane < HALO, right_part, jnp.where(lane >= width - HALO, left_part, 0.0))


def weights_kernel(place_ref, bound_ref, probe_ref, out_ref, sums_ref):
    modes = probe_ref.shape[0]
    width = probe_ref.shape[-1]
    half = width // 2
    rows = out_ref.shape[0]
    tile = rows - 2 * HALO
    power = jnp.zeros((width, width), jnp.float32)
    for m in range(modes):
        power += probe_ref[m, 0] * probe_ref[m, 0] + probe_ref[m, 1] * probe_ref[m, 1]
    sums_ref[...] = jnp.zeros_like(sums_ref)

    def place(frame, carry):
        row = place_ref[frame, 0]
        col = place_ref[frame, 1]

        @pl.when((row >= -width) & (row <= tile) & (col >= -width) & (col <= tile))
        def _():
            at_row = pl.ds(pl.multiple_of(row + width, half), width)
            at_col = pl.ds(pl.multiple_of(col + width, half), width)
            sums_ref[at_row, at_col] += power

        return carry

    lax.fori_loop(0, place_ref.shape[0], place, 0)
    low_row, high_row, low_col, high_col = (bound_ref[n] for n in range(4))

    chunk = 56

    def finish(step, carry):
        base = pl.multiple_of(step * chunk, 8)
        at = pl.ds(pl.multiple_of(base + width - HALO, 8), chunk)
        den = jnp.concatenate(
            [
                sums_ref[at, width : width + tile],
                edge_block(sums_ref[at, width + tile : width + tile + half], sums_ref[at, half:width]),
            ],
            axis=1,
        )
        row = lax.broadcasted_iota(jnp.int32, den.shape, 0) + (base - HALO)
        lane = lane_of(den.shape)
        col = jnp.where(lane >= tile + half - HALO, lane - (tile + half), lane)
        inside = (row >= low_row) & (row < high_row) & (col >= low_col) & (col < high_col)
        out_ref[pl.ds(base, chunk), :] = jnp.where(
            inside, 1.0 / (den + (obj_weight + 4.0 * smooth_weight)), 0.0
        )
        return carry

    lax.fori_loop(0, rows // chunk, finish, 0)


def object_weights(places, bounds, probe, tile):
    width = probe.shape[-1]
    smem = pl.BlockSpec(memory_space=pltpu.SMEM)
    return pl.pallas_call(
        weights_kernel,
        out_shape=jax.ShapeDtypeStruct((tile + 2 * HALO, tile + width // 2), jnp.float32),
        in_specs=[smem, smem, VMEM_SPEC],
        out_specs=VMEM_SPEC,
        scratch_shapes=[pltpu.VMEM((tile + 2 * width, tile + 2 * width), jnp.float32)],
        compiler_params=pltpu.CompilerParams(vmem_limit_bytes=VMEM_LIMIT),
        name="weights",
    )(places, bounds, probe)


def columns_kernel(
    lead_ref, trail_ref, last_ref, beyond_ref, head_ref, left_ref, right_ref, lead_out, trail_out, down_out, up_out
):
    half = lead_ref.shape[-1]
    tile = lead_ref.shape[1] - half
    for part in range(2):
        lead_out[part] = lead_ref[part] + left_ref[part, :, half:]
        trail_out[part] = edge_block(
            trail_ref[part] + right_ref[part], left_ref[part, :, :half]
        )
        down_out[part, :, :half] = lead_out[part, tile - HALO :, :]
        down_out[part, :HALO, half:tile] = last_ref[part, half - HALO :, half:tile]
        down_out[part, HALO:, half:tile] = beyond_ref[part, :, half:tile]
        down_out[part, :, tile:] = trail_out[part, tile - HALO :, :]
        up_out[part, :, :half] = lead_out[part, :HALO, :]
        up_out[part, :, half:tile] = head_ref[part, :, half:tile]
        up_out[part, :, tile:] = trail_out[part, :HALO, :]


def columns_sum(canvas, from_left, from_right):
    grow = canvas.shape[1]
    half = from_right.shape[-1]
    tile = grow - half
    strip = jax.ShapeDtypeStruct((2, grow, half), jnp.float32)
    return pl.pallas_call(
        columns_kernel,
        out_shape=(
            strip,
            strip,
            jax.ShapeDtypeStruct((2, half + HALO, grow), jnp.float32),
            jax.ShapeDtypeStruct((2, HALO, grow), jnp.float32),
        ),
        grid=(1,),
        in_specs=[
            pl.BlockSpec((2, grow, half), lambda g: (0, 0, 0)),
            pl.BlockSpec((2, grow, half), lambda g: (0, 0, tile // half)),
            pl.BlockSpec((2, half, grow), lambda g: (0, tile // half - 1, 0)),
            pl.BlockSpec((2, half, grow), lambda g: (0, tile // half, 0)),
            pl.BlockSpec((2, HALO, grow), lambda g: (0, 0, 0)),
            pl.BlockSpec((2, grow, 2 * half), lambda g: (0, 0, 0)),
            pl.BlockSpec((2, grow, half), lambda g: (0, 0, 0)),
        ],
        out_specs=[
            pl.BlockSpec((2, grow, half), lambda g: (0, 0, 0)),
            pl.BlockSpec((2, grow, half), lambda g: (0, 0, 0)),
            pl.BlockSpec((2, half + HALO, grow), lambda g: (0, 0, 0)),
            pl.BlockSpec((2, HALO, grow), lambda g: (0, 0, 0)),
        ],
        compiler_params=pltpu.CompilerParams(vmem_limit_bytes=VMEM_LIMIT),
        name="columns",
    )(canvas, canvas, canvas, canvas, canvas, from_left, from_right)


def sweeps_kernel(
    canvas_ref, lead_ref, trail_ref, above_ref, below_ref, obj_ref, top_ref, bottom_ref,
    left_ref, right_ref, weight_ref, field_ref, edge_ref, rhs_ref, first_ref, second_ref,
):
    tile = obj_ref.shape[1]
    half = lead_ref.shape[-1]
    rows = tile + 2 * HALO
    grow = tile + half
    chunk = 56
    for part in range(2):
        first_ref[part, :HALO, :tile] = top_ref[part]
        first_ref[part, HALO : HALO + tile, :tile] = obj_ref[part]
        first_ref[part, HALO + tile :, :tile] = bottom_ref[part]
        first_ref[part, :, tile:] = edge_block(right_ref[part], left_ref[part])
        rhs_ref[part, :HALO, :] = above_ref[part, :HALO, :]
        rhs_ref[part, HALO : HALO + tile, half:tile] = canvas_ref[part, :tile, half:tile]
        rhs_ref[part, HALO : HALO + tile, :half] = lead_ref[part, :tile, :]
        rhs_ref[part, HALO : HALO + tile, tile:] = trail_ref[part, :tile, :]
        rhs_ref[part, HALO + tile :, half:tile] = canvas_ref[part, tile : tile + HALO, half:tile]
        rhs_ref[part, HALO + tile :, :half] = lead_ref[part, tile : tile + HALO, :]
        rhs_ref[part, HALO + tile :, tile:] = trail_ref[part, tile : tile + HALO, :]
        rhs_ref[part, HALO + tile :, :] += below_ref[part]
        rhs_ref[part, HALO : HALO + half, :] += above_ref[part, HALO:, :]

        def prepare(step, carry):
            at = pl.ds(pl.multiple_of(step * chunk, 8), chunk)
            rhs_ref[part, at, :] = (
                rhs_ref[part, at, :] + obj_weight * first_ref[part, at, :]
            ) * weight_ref[at, :]
            return carry

        lax.fori_loop(0, rows // chunk, prepare, 0)

    def sweep(source, target, part):
        def step_rows(step, carry):
            base = pl.multiple_of(step * 8, 8)
            at = pl.ds(base, 8)
            before = pl.ds(pl.multiple_of(jnp.maximum(base - 8, 0), 8), 8)
            after = pl.ds(pl.multiple_of(jnp.minimum(base + 8, rows - 8), 8), 8)
            here = source[part, at, :]
            row = lax.broadcasted_iota(jnp.int32, here.shape, 0)
            up = jnp.where(row == 0, pltpu.roll(source[part, before, :], 1, 0), pltpu.roll(here, 1, 0))
            down = jnp.where(row == 7, pltpu.roll(source[part, after, :], 7, 0), pltpu.roll(here, 7, 0))
            sides = pltpu.roll(here, 1, 1) + pltpu.roll(here, grow - 1, 1)
            target[part, at, :] = rhs_ref[part, at, :] + (smooth_weight * weight_ref[at, :]) * (
                up + down + sides
            )
            return carry

        lax.fori_loop(0, rows // 8, step_rows, 0, unroll=2)

    for part in range(2):
        source, target = first_ref, second_ref
        for _ in range(SWEEPS):
            sweep(source, target, part)
            source, target = target, source
        field_ref[part] = source[part, HALO : HALO + tile, :tile]
        edge_ref[part] = source[part, HALO : HALO + tile, :half]


def object_sweeps(canvas, lead, trail, above, below, obj, top, bottom, left, right, weight):
    tile = obj.shape[1]
    grow = canvas.shape[1]
    rows = tile + 2 * HALO
    work = pltpu.VMEM((2, rows, grow), jnp.float32)
    return pl.pallas_call(
        sweeps_kernel,
        out_shape=(
            jax.ShapeDtypeStruct(obj.shape, jnp.float32),
            jax.ShapeDtypeStruct((2, tile, grow - tile), jnp.float32),
        ),
        in_specs=[VMEM_SPEC] * 11,
        out_specs=[VMEM_SPEC] * 2,
        scratch_shapes=[work, work, work],
        compiler_params=pltpu.CompilerParams(vmem_limit_bytes=VMEM_LIMIT),
        name="sweeps",
    )(canvas, lead, trail, above, below, obj, top, bottom, left, right, weight)


def windows_kernel(place_ref, field_ref, right_ref, below_ref, out_ref, whole_ref, load_sem, store_sem):
    tile = field_ref.shape[1]
    width = out_ref.shape[-1]
    half = width // 2
    loads = [
        pltpu.make_async_copy(field_ref, whole_ref.at[:, :tile, :tile], load_sem.at[0]),
        pltpu.make_async_copy(right_ref, whole_ref.at[:, :tile, tile:], load_sem.at[1]),
        pltpu.make_async_copy(below_ref, whole_ref.at[:, tile:, :], load_sem.at[2]),
    ]
    for copy in loads:
        copy.start()
    for copy in loads:
        copy.wait()
    stores = []
    for frame in range(out_ref.shape[0]):
        row = pl.multiple_of(place_ref[frame, 0], half)
        col = pl.multiple_of(place_ref[frame, 1], half)
        stores.append(
            pltpu.make_async_copy(
                whole_ref.at[:, pl.ds(row, width), pl.ds(col, width)], out_ref.at[frame], store_sem.at[frame]
            )
        )
    for copy in stores:
        copy.start()
    for copy in stores:
        copy.wait()


def windows(places, field, from_right, from_below, width):
    count = places.shape[0]
    grow = from_below.shape[-1]
    anywhere = pl.BlockSpec(memory_space=pl.ANY)
    return pl.pallas_call(
        windows_kernel,
        out_shape=jax.ShapeDtypeStruct((count, 2, width, width), jnp.float32),
        in_specs=[pl.BlockSpec(memory_space=pltpu.SMEM), anywhere, anywhere, anywhere],
        out_specs=anywhere,
        scratch_shapes=[
            pltpu.VMEM((2, grow, grow), jnp.float32),
            pltpu.SemaphoreType.DMA((3,)),
            pltpu.SemaphoreType.DMA((count,)),
        ],
        compiler_params=pltpu.CompilerParams(vmem_limit_bytes=VMEM_LIMIT),
        name="windows",
    )(places, field, from_right, from_below)


def halve(data, axis, mask):
    rows = data.shape[1] // 2
    upper = (lax.axis_index(axis) & mask) != 0
    keep = jnp.where(upper, rows, 0)
    give = jnp.where(upper, 0, rows)
    route = [(i, i ^ mask) for i in range(lax.axis_size(axis))]
    got = lax.ppermute(lax.dynamic_slice_in_dim(data, give, rows, axis=1), axis, route)
    return lax.dynamic_slice_in_dim(data, keep, rows, axis=1) + got


def double(data, axis, mask):
    upper = (lax.axis_index(axis) & mask) != 0
    route = [(i, i ^ mask) for i in range(lax.axis_size(axis))]
    got = lax.ppermute(data, axis, route)
    return jnp.concatenate([jnp.where(upper, got, data), jnp.where(upper, data, got)], axis=1)


def scatter_rows(data, axis):
    count = lax.axis_size(axis)
    rows = data.shape[1] // count
    me = lax.axis_index(axis)
    total = lax.dynamic_slice_in_dim(data, me * rows, rows, axis=1)
    for mask in range(1, count):
        route = [(i, i ^ mask) for i in range(count)]
        piece = lax.dynamic_slice_in_dim(data, (me ^ mask) * rows, rows, axis=1)
        total = total + lax.ppermute(piece, axis, route)
    return total


def gather_rows(data, axis):
    count = lax.axis_size(axis)
    rows = data.shape[1]
    me = lax.axis_index(axis)
    out = jnp.zeros((data.shape[0], rows * count) + data.shape[2:], data.dtype)
    out = lax.dynamic_update_slice_in_dim(out, data, me * rows, axis=1)
    for mask in range(1, count):
        route = [(i, i ^ mask) for i in range(count)]
        got = lax.ppermute(data, axis, route)
        out = lax.dynamic_update_slice_in_dim(out, got, (me ^ mask) * rows, axis=1)
    return out


def update_probe(num, probe):
    parts = num.shape[0] - 1
    width = probe.shape[-1]
    flat = probe.reshape(parts, width, width)
    cols, rows = lax.axis_size("col"), lax.axis_size("row")
    masks = [1 << n for n in range(cols.bit_length() - 1)]
    piece = num
    offset = jnp.zeros((), jnp.int32)
    span = width
    for mask in masks:
        piece = halve(piece, "col", mask)
        span = span // 2
        offset = offset + jnp.where((lax.axis_index("col") & mask) != 0, span, 0)
    piece = scatter_rows(piece, "row")
    span = span // rows
    offset = offset + lax.axis_index("row") * span
    mine = lax.dynamic_slice_in_dim(flat, offset, span, axis=1)
    fresh = (piece[:parts] + probe_weight * mine) / (piece[parts:] + probe_weight)
    fresh = gather_rows(fresh, "row")
    for mask in reversed(masks):
        fresh = double(fresh, "col", mask)
    return fresh.reshape(probe.shape)


def per_device(amplitude, patches, dual, probe, obj, positions):
    width = amplitude.shape[-1]
    half = width // 2
    tile = obj.shape[1]
    row_index = lax.axis_index("row")
    col_index = lax.axis_index("col")
    origin = jnp.stack([row_index * tile, col_index * tile]).astype(jnp.int32)
    places = positions - origin

    marked = positions + 1
    marked = jnp.concatenate([shift(marked, "col", 1), marked, shift(marked, "col", -1)], axis=0)
    marked = jnp.concatenate([shift(marked, "row", 1), marked, shift(marked, "row", -1)], axis=0)
    around = jnp.where(marked > 0, marked - 1 - origin, -tile * 4)
    bounds = jnp.stack(
        [
            -row_index * tile,
            (lax.axis_size("row") - row_index) * tile,
            -col_index * tile,
            (lax.axis_size("col") - col_index) * tile,
        ]
    ).astype(jnp.int32)
    weight = object_weights(around, bounds, probe, tile)

    top = shift(obj[:, tile - HALO :, :], "row", 1)
    bottom = shift(obj[:, :HALO, :], "row", -1)
    tall = jnp.concatenate([top, obj, bottom], axis=1)
    left = shift(tall[:, :, tile - half :], "col", 1)
    right = shift(tall[:, :, :half], "col", -1)

    dual_new, num, canvas = frames_update(amplitude, patches, dual, probe, places, tile)
    probe_new = update_probe(num, probe)

    from_left = shift(canvas[:, :, tile - half :], "col", 1)
    from_right = shift(canvas[:, :, :half], "col", -1)
    lead, trail, down, up = columns_sum(canvas, from_left, from_right)
    above = shift(down, "row", 1)
    below = shift(up, "row", -1)
    field, edge = object_sweeps(
        canvas, lead, trail, above, below, obj, top, bottom, left, right, weight
    )
    far_right = shift(edge, "col", -1)
    strip = jnp.concatenate([field[:, :half, :], far_right[:, :half, :]], axis=2)
    far_below = shift(strip, "row", -1)
    patches_new = windows(places, field, far_right, far_below, width)
    return (dual_new, field, probe_new, patches_new)


def solution(mesh):
    return jax.shard_map(
        per_device,
        mesh=mesh,
        in_specs=(
            P(("row", "col"), None, None),
            P(("row", "col"), None, None, None),
            P(("row", "col"), None, None, None, None),
            P(),
            P(None, "row", "col"),
            P(("row", "col"), None),
        ),
        out_specs=(
            P(("row", "col"), None, None, None, None),
            P(None, "row", "col"),
            P(),
            P(("row", "col"), None, None, None),
        ),
        check_vma=False,
    )
```

```python
import math

import jax
import jax.numpy as jnp
import numpy as np
from jax import lax
from jax.experimental import pallas as pl
from jax.experimental.pallas import tpu as pltpu
from jax.sharding import PartitionSpec as P


SWEEPS = 4
HALO = 8

amp_floor = 1.0
obj_weight = 0.5
smooth_weight = 16.0
probe_weight = 1.0

VMEM_SPEC = pl.BlockSpec(memory_space=pltpu.VMEM)
VMEM_LIMIT = 60 * 1024 * 1024


def shift(block, axis, distance):
    count = lax.axis_size(axis)
    route = [(i, i + distance) for i in range(count) if 0 <= i + distance < count]
    return lax.ppermute(block, axis, route)


def swap(block, axis, mask):
    return lax.ppermute(block, axis, [(i, i ^ mask) for i in range(lax.axis_size(axis))])


def split_two(value):
    high = value.astype(jnp.bfloat16)
    low = (value - high.astype(jnp.float32)).astype(jnp.bfloat16)
    return high, low


def dft_weights(width):
    half = width // 2
    k = np.arange(half)[:, None]
    j = np.arange(half)[None, :]
    mats = []
    for parity in range(2):
        angle = 2.0 * math.pi * ((k * (2 * j + parity)) % width) / width
        re = np.cos(angle) / math.sqrt(width)
        im = -np.sin(angle) / math.sqrt(width)
        mats.append(np.block([[re, im], [-im, re]]))
    pairs = []
    for m in mats + [m.T for m in mats]:
        high = m.astype(np.float32).astype(jnp.bfloat16)
        low = (m - high.astype(np.float64)).astype(np.float32).astype(jnp.bfloat16)
        pairs.append(np.stack([high, low]))
    order = np.concatenate([np.arange(0, width, 2), np.arange(1, width, 2)])
    perm = np.zeros((width, width), np.float32)
    perm[order, np.arange(width)] = 1.0
    return np.stack(pairs), perm.astype(jnp.bfloat16)


def mark_block(place_ref, origin, part, shape):
    lane = lane_of(shape)
    row = lax.broadcasted_iota(jnp.int32, shape, 0)
    block = jnp.zeros(shape, jnp.int32)
    for frame in range(place_ref.shape[0]):
        block = jnp.where((lane == frame) & (row == 0), place_ref[frame, part] + origin + 1, block)
    return block.astype(jnp.float32)


def lane_of(shape):
    return lax.broadcasted_iota(jnp.int32, shape, len(shape) - 1)


def edge_block(right_part, left_part):
    lane = lane_of(right_part.shape)
    width = right_part.shape[-1]
    return jnp.where(lane < HALO, right_part, jnp.where(lane >= width - HALO, left_part, 0.0))


def frames_kernel(
    place_ref, self_ref, amp_low_ref, amp_high_ref, patch_ref, dual_ref, probe_ref, pair_ref, perm_ref,
    obj_low_ref, obj_high_ref, obj_first_ref, obj_last_ref,
    new_ref, keep_ref, give_ref, canvas_ref, lead_ref, trail_ref, down_ref, up_ref,
    even_ref, odd_ref, num_ref, right_ref, left_ref,
):
    frame = pl.program_id(0)
    modes = probe_ref.shape[0]
    width = probe_ref.shape[-1]
    half = width // 2

    @pl.when(frame == 0)
    def _():
        canvas_ref[...] = jnp.zeros_like(canvas_ref)
        num_ref[...] = jnp.zeros_like(num_ref)
        for n in range(4):
            high, low = pair_ref[n, 0], pair_ref[n, 1]
            for k, m in enumerate((high, high, low)):
                right_ref[n, k * width : (k + 1) * width, :] = m
            for k, m in enumerate((high, low, high)):
                left_ref[(n + 2) % 4, :, k * width : (k + 1) * width] = m

    def dot(a, b):
        return jnp.dot(a, b, preferred_element_type=jnp.float32)

    def times_right(value, which):
        high, low = split_two(value)
        return dot(jnp.concatenate([high, low, high], axis=1), right_ref[which])

    def times_left(which, value):
        high, low = split_two(value)
        return dot(left_ref[which], jnp.concatenate([high, high, low], axis=0))

    patch_re = patch_ref[0, 0]
    patch_im = patch_ref[0, 1]

    def exit_wave(m):
        probe_re = probe_ref[m, 0]
        probe_im = probe_ref[m, 1]
        return probe_re * patch_re - probe_im * patch_im, probe_re * patch_im + probe_im * patch_re

    amps = []
    for parity in range(2):
        every = pl.ds(parity, half, stride=2)
        rows = jnp.concatenate([amp_low_ref[0, every, :], amp_high_ref[0, every, :]], axis=1)
        first = rows.astype(jnp.bfloat16)
        rest = rows - first.astype(jnp.float32)
        second, third = split_two(rest)
        amps.append(dot(first, perm_ref[...]) + (dot(second, perm_ref[...]) + dot(third, perm_ref[...])))

    power = [None, None]
    for m in range(modes):
        exit_re, exit_im = exit_wave(m)
        wave_re = exit_re + dual_ref[0, m, 0]
        wave_im = exit_im + dual_ref[0, m, 1]
        sums = jnp.concatenate(
            [wave_re[:, :half] + wave_re[:, half:], wave_im[:, :half] + wave_im[:, half:]], axis=1
        )
        diffs = jnp.concatenate(
            [wave_re[:, :half] - wave_re[:, half:], wave_im[:, :half] - wave_im[:, half:]], axis=1
        )
        even = times_right(sums, 0)
        odd = times_right(diffs, 1)

        def stack(op):
            return jnp.concatenate(
                [
                    jnp.concatenate([op(x[:half, part], x[half:, part]) for x in (even, odd)], axis=1)
                    for part in (slice(0, half), slice(half, width))
                ],
                axis=0,
            )

        far_even = times_left(0, stack(lambda a, b: a + b))
        far_odd = times_left(1, stack(lambda a, b: a - b))
        even_ref[m] = far_even
        odd_ref[m] = far_odd
        for parity, far in enumerate((far_even, far_odd)):
            term = far[:half] * far[:half] + far[half:] * far[half:]
            power[parity] = term if m == 0 else power[parity] + term

    ratios = []
    for parity in range(2):
        ratio = amps[parity] / jnp.sqrt(power[parity] + amp_floor)
        ratios.append(jnp.concatenate([ratio, ratio], axis=0))

    start_row = pl.multiple_of(place_ref[frame, 0], half)
    start_col = pl.multiple_of(place_ref[frame, 1], half)
    obj_re = jnp.zeros((width, width), jnp.float32)
    obj_im = jnp.zeros((width, width), jnp.float32)
    for m in range(modes):
        even = times_left(2, even_ref[m] * ratios[0])
        odd = times_left(3, odd_ref[m] * ratios[1])
        top = even + odd
        bottom = even - odd

        def rows_of(part):
            return jnp.concatenate(
                [
                    jnp.concatenate([x[:half, part], x[half:, part]], axis=1)
                    for x in (top, bottom)
                ],
                axis=0,
            )

        even = times_right(rows_of(slice(0, half)), 2)
        odd = times_right(rows_of(slice(half, width)), 3)
        low = even + odd
        high = even - odd
        near_re = jnp.concatenate([low[:, :half], high[:, :half]], axis=1)
        near_im = jnp.concatenate([low[:, half:], high[:, half:]], axis=1)
        exit_re, exit_im = exit_wave(m)
        new_re = dual_ref[0, m, 0] + exit_re - near_re
        new_im = dual_ref[0, m, 1] + exit_im - near_im
        new_ref[0, m, 0] = new_re
        new_ref[0, m, 1] = new_im
        target_re = near_re - new_re
        target_im = near_im - new_im
        num_ref[2 * m] += patch_re * target_re + patch_im * target_im
        num_ref[2 * m + 1] += patch_re * target_im - patch_im * target_re
        probe_re = probe_ref[m, 0]
        probe_im = probe_ref[m, 1]
        obj_re += probe_re * target_re + probe_im * target_im
        obj_im += probe_re * target_im - probe_im * target_re
    num_ref[2 * modes] += patch_re * patch_re + patch_im * patch_im
    canvas_ref[0, pl.ds(start_row, width), pl.ds(start_col, width)] += obj_re
    canvas_ref[1, pl.ds(start_row, width), pl.ds(start_col, width)] += obj_im

    @pl.when(frame == pl.num_programs(0) - 1)
    def _():
        grow = canvas_ref.shape[1]
        tile = grow - half
        blocks = grow // half
        kept = pl.multiple_of(self_ref[2] * half, half)
        given = pl.multiple_of((1 - self_ref[2]) * half, half)
        keep_ref[...] = num_ref[:, pl.ds(kept, half), :]
        give_ref[...] = num_ref[:, pl.ds(given, half), :]
        for part in range(2):
            origin = self_ref[part] * tile
            lead_ref[part, :grow, :] = canvas_ref[part, :, tile:]
            down_ref[part, : half + HALO, :] = canvas_ref[part, tile - HALO :, :]
            up_ref[part, :HALO, :] = canvas_ref[part, :HALO, :]
            ends = edge_block(canvas_ref[part, :, :half], canvas_ref[part, :, tile - half : tile]).T
            for n in range(blocks):
                at = slice(n * half, (n + 1) * half)
                trail_ref[part, n * HALO : (n + 1) * HALO, :] = ends[:HALO, at]
                lead_ref[part, grow + n * HALO : grow + (n + 1) * HALO, :] = ends[half - HALO :, at]
            ends = edge_block(obj_low_ref[part], obj_high_ref[part]).T
            for n in range(blocks - 1):
                at = slice(n * half, (n + 1) * half)
                to = (blocks + n) * HALO
                trail_ref[part, to : to + HALO, :] = ends[:HALO, at]
                lead_ref[part, grow + to : grow + to + HALO, :] = ends[half - HALO :, at]
            note = mark_block(place_ref, origin, part, (HALO, half))
            to = (2 * blocks - 1) * HALO
            trail_ref[part, to:, :] = note
            lead_ref[part, grow + to :, :] = note
            down_ref[part, half + HALO : half + 2 * HALO, :tile] = obj_last_ref[part]
            up_ref[part, HALO : 2 * HALO, :tile] = obj_first_ref[part]
            for ref, at in ((down_ref, half + 2 * HALO), (up_ref, 2 * HALO)):
                ref[part, at - HALO : at, tile:] = jnp.zeros((HALO, half), jnp.float32)
                ref[part, at:, :half] = note
                ref[part, at:, half:] = jnp.zeros((HALO, tile), jnp.float32)


def frames_update(amplitude, patches, dual, probe, obj, places, self_index):
    count, modes = dual.shape[:2]
    width = amplitude.shape[-1]
    pairs, perm = dft_weights(width)
    half = width // 2
    tile = obj.shape[1]
    grow = tile + half
    notes = 2 * grow // half * HALO
    last = tile // half - 1
    messages = (
        (2 * modes + 1, half, width),
        (2 * modes + 1, half, width),
        (2, grow, grow),
        (2, grow + notes, half),
        (2, notes, half),
        (2, half + 3 * HALO, grow),
        (2, 3 * HALO, grow),
    )

    def whole(shape):
        return pl.BlockSpec(shape, lambda f, *_: (0,) * len(shape))

    return pl.pallas_call(
        frames_kernel,
        out_shape=(jax.ShapeDtypeStruct(dual.shape, jnp.float32),)
        + tuple(jax.ShapeDtypeStruct(m, jnp.float32) for m in messages),
        grid_spec=pltpu.PrefetchScalarGridSpec(
            num_scalar_prefetch=2,
            grid=(count,),
            in_specs=[
                pl.BlockSpec((1, width, half), lambda f, *_: (f, 0, 0)),
                pl.BlockSpec((1, width, half), lambda f, *_: (f, 0, 1)),
                pl.BlockSpec((1, 2, width, width), lambda f, *_: (f, 0, 0, 0)),
                pl.BlockSpec((1, modes, 2, width, width), lambda f, *_: (f, 0, 0, 0, 0)),
                whole(probe.shape),
                whole(pairs.shape),
                whole(perm.shape),
                pl.BlockSpec((2, tile, half), lambda f, *_: (0, 0, 0)),
                pl.BlockSpec((2, tile, half), lambda f, *_: (0, 0, last)),
                pl.BlockSpec((2, HALO, tile), lambda f, *_: (0, 0, 0)),
                pl.BlockSpec((2, HALO, tile), lambda f, *_: (0, tile // HALO - 1, 0)),
            ],
            out_specs=[
                pl.BlockSpec((1, modes, 2, width, width), lambda f, *_: (f, 0, 0, 0, 0)),
            ]
            + [whole(m) for m in messages],
            scratch_shapes=[
                pltpu.VMEM((modes, width, width), jnp.float32),
                pltpu.VMEM((modes, width, width), jnp.float32),
                pltpu.VMEM((2 * modes + 1, width, width), jnp.float32),
                pltpu.VMEM((4, 3 * width, width), jnp.bfloat16),
                pltpu.VMEM((4, width, 3 * width), jnp.bfloat16),
            ],
        ),
        compiler_params=pltpu.CompilerParams(vmem_limit_bytes=VMEM_LIMIT),
        cost_estimate=pl.CostEstimate(
            flops=count * modes * 24 * 2 * width**3, bytes_accessed=20 << 20, transcendentals=0
        ),
        name="frames",
    )(
        places, self_index, amplitude, amplitude, patches, dual, probe,
        jnp.asarray(pairs), jnp.asarray(perm), obj, obj, obj, obj,
    )


def weights_kernel(place_ref, bound_ref, probe_ref, out_ref, sums_ref):
    modes = probe_ref.shape[0]
    width = probe_ref.shape[-1]
    half = width // 2
    rows = out_ref.shape[1]
    tile = rows - 2 * HALO
    power = jnp.zeros((width, width), jnp.float32)
    for m in range(modes):
        power += probe_ref[m, 0] * probe_ref[m, 0] + probe_ref[m, 1] * probe_ref[m, 1]
    sums_ref[...] = jnp.zeros_like(sums_ref)

    def place(frame, carry):
        row = place_ref[frame, 0]
        col = place_ref[frame, 1]

        @pl.when((row >= -width) & (row <= tile) & (col >= -width) & (col <= tile))
        def _():
            at_row = pl.ds(pl.multiple_of(row + width, half), width)
            at_col = pl.ds(pl.multiple_of(col + width, half), width)
            sums_ref[at_row, at_col] += power

        return carry

    lax.fori_loop(0, place_ref.shape[0], place, 0)
    low_row, high_row, low_col, high_col = (bound_ref[n] for n in range(4))

    chunk = 56

    def finish(step, carry):
        base = pl.multiple_of(step * chunk, 8)
        at = pl.ds(pl.multiple_of(base + width - HALO, 8), chunk)
        den = jnp.concatenate(
            [
                sums_ref[at, width : width + tile],
                edge_block(sums_ref[at, width + tile : width + tile + half], sums_ref[at, half:width]),
            ],
            axis=1,
        )
        row = lax.broadcasted_iota(jnp.int32, den.shape, 0) + (base - HALO)
        lane = lane_of(den.shape)
        col = jnp.where(lane >= tile + half - HALO, lane - (tile + half), lane)
        inside = (row >= low_row) & (row < high_row) & (col >= low_col) & (col < high_col)
        ratio = jnp.where(inside, smooth_weight / (den + (obj_weight + 4.0 * smooth_weight)), 0.0)
        for n in range(out_ref.shape[0]):
            out_ref[n, pl.ds(base, chunk), :] = ratio[:, n * half : (n + 1) * half]
        return carry

    lax.fori_loop(0, rows // chunk, finish, 0)


def object_weights(places, bounds, probe, tile):
    width = probe.shape[-1]
    smem = pl.BlockSpec(memory_space=pltpu.SMEM)
    return pl.pallas_call(
        weights_kernel,
        out_shape=jax.ShapeDtypeStruct(
            (2 * tile // width + 1, tile + 2 * HALO, width // 2), jnp.float32
        ),
        in_specs=[smem, smem, VMEM_SPEC],
        out_specs=VMEM_SPEC,
        scratch_shapes=[pltpu.VMEM((tile + 2 * width, tile + 2 * width), jnp.float32)],
        compiler_params=pltpu.CompilerParams(vmem_limit_bytes=VMEM_LIMIT),
        name="weights",
    )(places, bounds, probe)


PAD = 8


def sweeps_kernel(
    canvas_ref, lead_ref, trail_ref, above_ref, below_ref, corner_above_ref, corner_below_ref,
    obj_ref, weight_ref, *refs,
):
    field_ref, edge_ref, head_ref, rhs_ref, first_ref, second_ref = refs[-6:]
    tile = obj_ref.shape[1]
    half = lead_ref.shape[-1]
    rows = tile + 2 * HALO
    grow = tile + half
    blocks = grow // half
    wide = blocks - 1
    chunk = 56
    tall = half + HALO
    own = slice(PAD + HALO, PAD + HALO + tile)
    upper = slice(PAD, PAD + HALO)
    lower = slice(PAD + HALO + tile, PAD + 2 * HALO + tile)
    near_top = slice(PAD + HALO, PAD + HALO + half)
    lane = lane_of((rows, half))

    def thin(ref, start, count):
        return jnp.concatenate(
            [ref[0, start + n * HALO : start + (n + 1) * HALO, :] for n in range(count)], axis=1
        )

    def halo(middle, above, below):
        return jnp.concatenate(
            [above[:, :half], middle[:, :half] + above[:, half:], middle[:, half:tile], middle[:, tile:] + below],
            axis=1,
        )

    def columns(right_halo, left_halo):
        gap = jnp.zeros((half - 2 * HALO, right_halo.shape[1]), jnp.float32)
        return jnp.concatenate([right_halo, gap, left_halo], axis=0).T[half - HALO : half + tile + HALO]

    nothing = jnp.zeros((HALO, half), jnp.float32)
    sides = columns(
        halo(
            thin(trail_ref, 0, blocks),
            thin(corner_above_ref, tall + 4 * HALO, 2),
            corner_below_ref[0, 4 * HALO : 5 * HALO, :],
        ),
        halo(
            thin(lead_ref, grow, blocks),
            thin(corner_above_ref, tall, 2),
            corner_below_ref[0, HALO : 2 * HALO, :],
        ),
    )
    first_ref[wide, PAD : PAD + rows, :] = columns(
        halo(
            jnp.concatenate([thin(trail_ref, blocks * HALO, blocks - 1), nothing], axis=1),
            jnp.concatenate([corner_above_ref[0, tall + 6 * HALO : tall + 7 * HALO, :], nothing], axis=1),
            corner_below_ref[0, 5 * HALO : 6 * HALO, :],
        ),
        halo(
            jnp.concatenate([thin(lead_ref, grow + blocks * HALO, blocks - 1), nothing], axis=1),
            jnp.concatenate([corner_above_ref[0, tall + 2 * HALO : tall + 3 * HALO, :], nothing], axis=1),
            corner_below_ref[0, 2 * HALO : 3 * HALO, :],
        ),
    )
    for n in range(blocks):
        at = slice(n * half, (n + 1) * half)
        if n < wide:
            first_ref[n, upper, :] = above_ref[0, tall : tall + HALO, at]
            first_ref[n, own, :] = obj_ref[0, :, at]
            first_ref[n, lower, :] = below_ref[0, HALO : 2 * HALO, at]
        rhs_ref[n, upper, :] = above_ref[0, :HALO, at]
        rhs_ref[n, own, :] = canvas_ref[0, :tile, at]
        rhs_ref[n, lower, :] = canvas_ref[0, tile : tile + HALO, at] + below_ref[0, :HALO, at]
        rhs_ref[n, near_top, :] += above_ref[0, HALO:tall, at]
        for ref in (first_ref, second_ref):
            ref[n, :PAD, :] = jnp.zeros((PAD, half), jnp.float32)
            ref[n, PAD + rows :, :] = jnp.zeros((PAD, half), jnp.float32)
    rhs_ref[0, PAD + HALO : PAD + 2 * HALO + tile, :] += lead_ref[0, : tile + HALO, :]
    rhs_ref[0, PAD : PAD + tall, :] += corner_above_ref[0, :tall, :]
    rhs_ref[0, lower, :] += corner_below_ref[0, :HALO, :]
    rhs_ref[wide, PAD : PAD + rows, :] = sides + jnp.where(
        lane < HALO, rhs_ref[wide, PAD : PAD + rows, :], 0.0
    )

    def prepare(step, carry):
        base = pl.multiple_of(step * chunk, 8)
        for n in range(blocks):
            at = pl.ds(base + PAD, chunk)
            rhs_ref[n, at, :] = (rhs_ref[n, at, :] + obj_weight * first_ref[n, at, :]) * (
                weight_ref[n, pl.ds(base, chunk), :] * (1.0 / smooth_weight)
            )
        return carry

    lax.fori_loop(0, rows // chunk, prepare, 0)
    narrow = lane_of((8, half))
    stride = 2 * chunk

    def sweep(source, target):
        def step_rows(step, carry):
            base = pl.multiple_of(step * stride, 8)

            def turned(group):
                at = pl.ds(base + (PAD + 8 * group), 8)
                mids = [source[n, at, :] for n in range(blocks)]
                return [pltpu.roll(m, 1, 1) for m in mids], [pltpu.roll(m, half - 1, 1) for m in mids]

            ahead = turned(0)
            for group in range(stride // 8):
                froms, tos = ahead
                if group + 1 < stride // 8:
                    ahead = turned(group + 1)
                here = base + (PAD + 8 * group)
                for n in range(blocks):
                    west = jnp.where(narrow == 0, froms[n - 1], froms[n])
                    east = jnp.where(narrow == half - 1, tos[(n + 1) % blocks], tos[n])
                    north = source[n, pl.ds(here - 1, 8), :]
                    south = source[n, pl.ds(here + 1, 8), :]
                    target[n, pl.ds(here, 8), :] = rhs_ref[n, pl.ds(here, 8), :] + weight_ref[
                        n, pl.ds(base + 8 * group, 8), :
                    ] * ((north + south) + (west + east))
            return carry

        lax.fori_loop(0, rows // stride, step_rows, 0)

    source, target = first_ref, second_ref
    for _ in range(SWEEPS):
        sweep(source, target)
        source, target = target, source
    for n in range(wide):
        at = slice(n * half, (n + 1) * half)
        field_ref[0, :, at] = source[n, own, :]
        head_ref[0, :, at] = source[n, near_top, :]
    edge_ref[0] = source[0, own, :]


def object_sweeps(part, canvas, lead, trail, above, below, corner_above, corner_below, obj, weight, field):
    tile = obj.shape[1]
    half = lead.shape[-1]
    work = pltpu.VMEM((tile // half + 1, tile + 2 * HALO + 2 * PAD, half), jnp.float32)
    sources = [canvas, lead, trail, above, below, corner_above, corner_below, obj]

    def one(shape):
        return pl.BlockSpec((1,) + tuple(shape[1:]), lambda g: (part, 0, 0))

    extra = [] if field is None else [field]
    return pl.pallas_call(
        sweeps_kernel,
        out_shape=(
            jax.ShapeDtypeStruct(obj.shape, jnp.float32),
            jax.ShapeDtypeStruct((1, tile, half), jnp.float32),
            jax.ShapeDtypeStruct((1, half, tile), jnp.float32),
        ),
        grid=(1,),
        in_specs=[one(x.shape) for x in sources]
        + [pl.BlockSpec(weight.shape, lambda g: (0, 0, 0))]
        + [pl.BlockSpec(memory_space=pl.ANY)] * len(extra),
        out_specs=[
            one(obj.shape),
            pl.BlockSpec((1, tile, half), lambda g: (0, 0, 0)),
            pl.BlockSpec((1, half, tile), lambda g: (0, 0, 0)),
        ],
        scratch_shapes=[work, work, work],
        input_output_aliases={9: 0} if extra else {},
        compiler_params=pltpu.CompilerParams(vmem_limit_bytes=VMEM_LIMIT),
    )(*sources, weight, *extra)


def windows_kernel(place_ref, field_ref, *refs):
    strips = refs[:6]
    out_ref, whole_ref, load_sem, store_sem = refs[6:]
    tile = field_ref.shape[1]
    width = out_ref.shape[-1]
    half = width // 2
    loads = [pltpu.make_async_copy(field_ref, whole_ref.at[:, :tile, :tile], load_sem.at[0])]
    for part in range(2):
        spots = (
            whole_ref.at[part, :tile, tile:],
            whole_ref.at[part, tile:, :tile],
            whole_ref.at[part, tile:, tile:],
        )
        for n, spot in enumerate(spots):
            loads.append(
                pltpu.make_async_copy(strips[3 * part + n].at[0], spot, load_sem.at[1 + 3 * part + n])
            )
    for copy in loads:
        copy.start()
    for copy in loads:
        copy.wait()
    stores = []
    for frame in range(out_ref.shape[0]):
        row = pl.multiple_of(place_ref[frame, 0], half)
        col = pl.multiple_of(place_ref[frame, 1], half)
        stores.append(
            pltpu.make_async_copy(
                whole_ref.at[:, pl.ds(row, width), pl.ds(col, width)], out_ref.at[frame], store_sem.at[frame]
            )
        )
    for copy in stores:
        copy.start()
    for copy in stores:
        copy.wait()


def windows(places, field, strips, width):
    count = places.shape[0]
    grow = field.shape[1] + width // 2
    anywhere = pl.BlockSpec(memory_space=pl.ANY)
    return pl.pallas_call(
        windows_kernel,
        out_shape=jax.ShapeDtypeStruct((count, 2, width, width), jnp.float32),
        in_specs=[pl.BlockSpec(memory_space=pltpu.SMEM)] + [anywhere] * 7,
        out_specs=anywhere,
        scratch_shapes=[
            pltpu.VMEM((2, grow, grow), jnp.float32),
            pltpu.SemaphoreType.DMA((7,)),
            pltpu.SemaphoreType.DMA((count,)),
        ],
        compiler_params=pltpu.CompilerParams(vmem_limit_bytes=VMEM_LIMIT),
        name="windows",
    )(places, field, *strips)


def halve(data, axis, mask):
    rows = data.shape[1] // 2
    upper = (lax.axis_index(axis) & mask) != 0
    keep = jnp.where(upper, rows, 0)
    give = jnp.where(upper, 0, rows)
    got = swap(lax.dynamic_slice_in_dim(data, give, rows, axis=1), axis, mask)
    return lax.dynamic_slice_in_dim(data, keep, rows, axis=1) + got


def double(data, axis, mask):
    upper = (lax.axis_index(axis) & mask) != 0
    got = swap(data, axis, mask)
    return jnp.concatenate([jnp.where(upper, got, data), jnp.where(upper, data, got)], axis=1)


def probe_steps():
    cols, rows = lax.axis_size("col"), lax.axis_size("row")
    steps = [("col", 1 << n) for n in range(cols.bit_length() - 1)]
    return steps + [("row", 1 << n) for n in (0, *reversed(range(1, rows.bit_length() - 1)))]


def update_probe(keep, give, probe):
    parts = keep.shape[0] - 1
    width = probe.shape[-1]
    flat = probe.reshape(parts, width, width)
    steps = probe_steps()
    piece = keep + swap(give, *steps[0])
    offset = jnp.zeros((), jnp.int32)
    span = width
    for n, (axis, mask) in enumerate(steps):
        if n > 0:
            piece = halve(piece, axis, mask)
        span = span // 2
        offset = offset + jnp.where((lax.axis_index(axis) & mask) != 0, span, 0)
    mine = lax.dynamic_slice_in_dim(flat, offset, span, axis=1)
    fresh = (piece[:parts] + probe_weight * mine) / (piece[parts:] + probe_weight)
    for n, (axis, mask) in reversed(list(enumerate(steps))):
        fresh = double(fresh, axis, mask)
    return fresh.reshape(probe.shape)


def per_device(amplitude, patches, dual, probe, obj, positions):
    width = amplitude.shape[-1]
    half = width // 2
    tile = obj.shape[1]
    count = positions.shape[0]
    row_index = lax.axis_index("row")
    col_index = lax.axis_index("col")
    origin = jnp.stack([row_index * tile, col_index * tile]).astype(jnp.int32)
    places = positions - origin
    self_index = jnp.stack([row_index, col_index, col_index & 1]).astype(jnp.int32)

    dual_new, keep, give, canvas, lead, trail, down, up = frames_update(
        amplitude, patches, dual, probe, obj, places, self_index
    )
    lead = shift(lead, "col", 1)
    trail = shift(trail, "col", -1)
    above = shift(down, "row", 1)
    below = shift(up, "row", -1)
    grow = tile + half
    blocks = grow // half
    notes = (2 * blocks - 1) * HALO
    corner_down = jnp.concatenate(
        [
            lead[:, tile - HALO : grow],
            lead[:, grow + (blocks - 2) * HALO : grow + blocks * HALO],
            lead[:, grow + notes - HALO :],
            trail[:, (blocks - 2) * HALO : blocks * HALO],
            trail[:, notes - HALO :],
        ],
        axis=1,
    )
    corner_up = jnp.concatenate(
        [
            lead[:, :HALO],
            lead[:, grow : grow + HALO],
            lead[:, grow + blocks * HALO : grow + (blocks + 1) * HALO],
            lead[:, grow + notes :],
            trail[:, :HALO],
            trail[:, blocks * HALO : (blocks + 1) * HALO],
            trail[:, notes:],
        ],
        axis=1,
    )
    corner_above = shift(corner_down, "row", 1)
    corner_below = shift(corner_up, "row", -1)
    tall = half + HALO
    own_marks = (positions + 1).astype(jnp.float32).T
    marks = jnp.concatenate(
        [
            own_marks,
            lead[:, grow + notes, :count],
            trail[:, notes, :count],
            above[:, tall + HALO, :count],
            below[:, 2 * HALO, :count],
            corner_above[:, tall + 3 * HALO, :count],
            corner_above[:, tall + 7 * HALO, :count],
            corner_below[:, 3 * HALO, :count],
            corner_below[:, 6 * HALO, :count],
        ],
        axis=1,
    )
    marks = marks.T.astype(jnp.int32)
    around = jnp.where(marks > 0, marks - 1 - origin, -tile * 4)
    bounds = jnp.stack(
        [
            -row_index * tile,
            (lax.axis_size("row") - row_index) * tile,
            -col_index * tile,
            (lax.axis_size("col") - col_index) * tile,
        ]
    ).astype(jnp.int32)
    weight = object_weights(around, bounds, probe, tile)
    field = None
    strips = []
    for part in range(2):
        field, edge, head = object_sweeps(
            part, canvas, lead, trail, above, below, corner_above, corner_below, obj, weight, field
        )
        far_below = shift(head, "row", -1)
        far_right = shift(edge, "col", -1)
        far_corner = shift(far_right[:, :half, :], "row", -1)
        strips += [far_right, far_below, far_corner]
    probe_new = update_probe(keep, give, probe)
    patches_new = windows(places, field, strips, width)
    return (dual_new, field, probe_new, patches_new)


def solution(mesh):
    return jax.shard_map(
        per_device,
        mesh=mesh,
        in_specs=(
            P(("row", "col"), None, None),
            P(("row", "col"), None, None, None),
            P(("row", "col"), None, None, None, None),
            P(),
            P(None, "row", "col"),
            P(("row", "col"), None),
        ),
        out_specs=(
            P(("row", "col"), None, None, None, None),
            P(None, "row", "col"),
            P(),
            P(("row", "col"), None, None, None),
        ),
        check_vma=False,
    )
```

```python
import functools
import math

import jax
import jax.numpy as jnp
import numpy as np
from jax import lax
from jax.experimental import pallas as pl
from jax.experimental.pallas import tpu as pltpu
from jax.sharding import PartitionSpec as P


SWEEPS = 4
HALO = 8

amp_floor = 1.0
obj_weight = 0.5
smooth_weight = 16.0
probe_weight = 1.0

VMEM_SPEC = pl.BlockSpec(memory_space=pltpu.VMEM)
VMEM_LIMIT = 60 * 1024 * 1024


def shift(block, axis, distance):
    count = lax.axis_size(axis)
    route = [(i, i + distance) for i in range(count) if 0 <= i + distance < count]
    return lax.ppermute(block, axis, route)


def swap(block, row_mask, col_mask):
    rows, cols = lax.axis_size("row"), lax.axis_size("col")
    route = [
        (r * cols + c, (r ^ row_mask) * cols + (c ^ col_mask)) for r in range(rows) for c in range(cols)
    ]
    return lax.ppermute(block, ("row", "col"), route)


def split_two(value):
    high = value.astype(jnp.bfloat16)
    low = (value - high.astype(jnp.float32)).astype(jnp.bfloat16)
    return high, low


def dft_weights(width):
    half = width // 2
    k = np.arange(half)[:, None]
    j = np.arange(half)[None, :]
    mats = []
    for parity in range(2):
        angle = 2.0 * math.pi * ((k * (2 * j + parity)) % width) / width
        re = np.cos(angle) / math.sqrt(width)
        im = -np.sin(angle) / math.sqrt(width)
        mats.append(np.block([[re, im], [-im, re]]))
    pairs = []
    for m in mats + [m.T for m in mats]:
        high = m.astype(np.float32).astype(jnp.bfloat16)
        low = (m - high.astype(np.float64)).astype(np.float32).astype(jnp.bfloat16)
        pairs.append(np.stack([high, low]))
    order = np.concatenate([np.arange(0, width, 2), np.arange(1, width, 2)])
    perm = np.zeros((width, width), np.float32)
    perm[order, np.arange(width)] = 1.0
    return np.stack(pairs), perm.astype(jnp.bfloat16)


def lane_of(shape):
    return lax.broadcasted_iota(jnp.int32, shape, len(shape) - 1)


def edge_block(right_part, left_part):
    lane = lane_of(right_part.shape)
    width = right_part.shape[-1]
    return jnp.where(lane < HALO, right_part, jnp.where(lane >= width - HALO, left_part, 0.0))


def frames_kernel(
    place_ref, self_ref, amp_low_ref, amp_high_ref, patch_ref, dual_ref, probe_ref, pair_ref, perm_ref,
    obj_low_ref, obj_high_ref, obj_first_ref, obj_last_ref,
    new_ref, keep_ref, give_ref, canvas_ref, lead_ref, link_ref, trail_ref, down0_ref, down1_ref, up_ref,
    even_ref, odd_ref, num_ref, right_ref, left_ref,
):
    frame = pl.program_id(0)
    modes = probe_ref.shape[0]
    width = probe_ref.shape[-1]
    half = width // 2

    @pl.when(frame == 0)
    def _():
        canvas_ref[...] = jnp.zeros_like(canvas_ref)
        num_ref[...] = jnp.zeros_like(num_ref)
        for n in range(4):
            high, low = pair_ref[n, 0], pair_ref[n, 1]
            for k, m in enumerate((high, high, low)):
                right_ref[n, k * width : (k + 1) * width, :] = m
            for k, m in enumerate((high, low, high)):
                left_ref[(n + 2) % 4, :, k * width : (k + 1) * width] = m

    def dot(a, b):
        return jnp.dot(a, b, preferred_element_type=jnp.float32)

    def times_right(value, which):
        high, low = split_two(value)
        return dot(jnp.concatenate([high, low, high], axis=1), right_ref[which])

    def times_left(which, value):
        high, low = split_two(value)
        return dot(left_ref[which], jnp.concatenate([high, high, low], axis=0))

    patch_re = patch_ref[0, 0]
    patch_im = patch_ref[0, 1]

    def exit_wave(m):
        probe_re = probe_ref[m, 0]
        probe_im = probe_ref[m, 1]
        return probe_re * patch_re - probe_im * patch_im, probe_re * patch_im + probe_im * patch_re

    amps = []
    for parity in range(2):
        every = pl.ds(parity, half, stride=2)
        rows = jnp.concatenate([amp_low_ref[0, every, :], amp_high_ref[0, every, :]], axis=1)
        first = rows.astype(jnp.bfloat16)
        rest = rows - first.astype(jnp.float32)
        second, third = split_two(rest)
        amps.append(dot(first, perm_ref[...]) + (dot(second, perm_ref[...]) + dot(third, perm_ref[...])))

    power = [None, None]
    for m in range(modes):
        exit_re, exit_im = exit_wave(m)
        wave_re = exit_re + dual_ref[0, m, 0]
        wave_im = exit_im + dual_ref[0, m, 1]
        sums = jnp.concatenate(
            [wave_re[:, :half] + wave_re[:, half:], wave_im[:, :half] + wave_im[:, half:]], axis=1
        )
        diffs = jnp.concatenate(
            [wave_re[:, :half] - wave_re[:, half:], wave_im[:, :half] - wave_im[:, half:]], axis=1
        )
        even = times_right(sums, 0)
        odd = times_right(diffs, 1)

        def stack(op):
            return jnp.concatenate(
                [
                    jnp.concatenate([op(x[:half, part], x[half:, part]) for x in (even, odd)], axis=1)
                    for part in (slice(0, half), slice(half, width))
                ],
                axis=0,
            )

        far_even = times_left(0, stack(lambda a, b: a + b))
        far_odd = times_left(1, stack(lambda a, b: a - b))
        even_ref[m] = far_even
        odd_ref[m] = far_odd
        for parity, far in enumerate((far_even, far_odd)):
            term = far[:half] * far[:half] + far[half:] * far[half:]
            power[parity] = term if m == 0 else power[parity] + term

    ratios = []
    for parity in range(2):
        ratio = amps[parity] / jnp.sqrt(power[parity] + amp_floor)
        ratios.append(jnp.concatenate([ratio, ratio], axis=0))

    tile = canvas_ref.shape[1] - half
    start_row = pl.multiple_of(place_ref[frame, 0] - self_ref[0] * tile, half)
    start_col = pl.multiple_of(place_ref[frame, 1] - self_ref[1] * tile, half)
    obj_re = jnp.zeros((width, width), jnp.float32)
    obj_im = jnp.zeros((width, width), jnp.float32)
    for m in range(modes):
        even = times_left(2, even_ref[m] * ratios[0])
        odd = times_left(3, odd_ref[m] * ratios[1])
        top = even + odd
        bottom = even - odd

        def rows_of(part):
            return jnp.concatenate(
                [
                    jnp.concatenate([x[:half, part], x[half:, part]], axis=1)
                    for x in (top, bottom)
                ],
                axis=0,
            )

        even = times_right(rows_of(slice(0, half)), 2)
        odd = times_right(rows_of(slice(half, width)), 3)
        low = even + odd
        high = even - odd
        near_re = jnp.concatenate([low[:, :half], high[:, :half]], axis=1)
        near_im = jnp.concatenate([low[:, half:], high[:, half:]], axis=1)
        exit_re, exit_im = exit_wave(m)
        new_re = dual_ref[0, m, 0] + exit_re - near_re
        new_im = dual_ref[0, m, 1] + exit_im - near_im
        new_ref[0, m, 0] = new_re
        new_ref[0, m, 1] = new_im
        target_re = near_re - new_re
        target_im = near_im - new_im
        num_ref[2 * m] += patch_re * target_re + patch_im * target_im
        num_ref[2 * m + 1] += patch_re * target_im - patch_im * target_re
        probe_re = probe_ref[m, 0]
        probe_im = probe_ref[m, 1]
        obj_re += probe_re * target_re + probe_im * target_im
        obj_im += probe_re * target_im - probe_im * target_re
    num_ref[2 * modes] += patch_re * patch_re + patch_im * patch_im
    canvas_ref[0, pl.ds(start_row, width), pl.ds(start_col, width)] += obj_re
    canvas_ref[1, pl.ds(start_row, width), pl.ds(start_col, width)] += obj_im

    @pl.when(frame == pl.num_programs(0) - 1)
    def _():
        grow = canvas_ref.shape[1]
        blocks = grow // half
        kept = pl.multiple_of((self_ref[1] & 1) * half, half)
        given = pl.multiple_of((1 - (self_ref[1] & 1)) * half, half)
        keep_ref[...] = num_ref[:, pl.ds(kept, half), :]
        give_ref[...] = num_ref[:, pl.ds(given, half), :]
        shape = (HALO, half)
        lane = lane_of(shape)
        row = lax.broadcasted_iota(jnp.int32, shape, 0)
        marks = jnp.zeros(shape, jnp.int32)
        for n in range(place_ref.shape[0]):
            for part in range(2):
                marks = jnp.where((lane == n) & (row == part), place_ref[n, part] + 1, marks)
        marks = marks.astype(jnp.float32)
        for part, down_ref in enumerate((down0_ref, down1_ref)):
            down_ref[: half + HALO, :] = canvas_ref[part, tile - HALO :, :]
            down_ref[half + HALO : half + 2 * HALO, :tile] = obj_last_ref[part]
            down_ref[half + HALO : half + 2 * HALO, tile:] = jnp.zeros(shape, jnp.float32)
            lead_ref[part] = canvas_ref[part, :, tile:]
            link_ref[part, : half + HALO, :] = canvas_ref[part, tile - HALO :, tile:]
            link_ref[part, half + HALO : half + 2 * HALO, :] = canvas_ref[part, :HALO, tile:]
            past = half + 2 * HALO
            up_ref[part, :HALO, :] = canvas_ref[part, :HALO, :]
            up_ref[part, HALO:, :tile] = obj_first_ref[part]
            up_ref[part, HALO:, tile:] = marks
            sums = edge_block(canvas_ref[part, :, :half], canvas_ref[part, :, tile - half : tile]).T
            objs = edge_block(obj_low_ref[part], obj_high_ref[part]).T
            for ends, count, base in ((sums, blocks, 0), (objs, blocks - 1, blocks)):
                for n in range(count):
                    at = slice(n * half, (n + 1) * half)
                    to = (base + n) * HALO
                    trail_ref[part, to : to + HALO, :] = ends[:HALO, at]
                    link_ref[part, past + to : past + to + HALO, :] = ends[half - HALO :, at]
            to = (2 * blocks - 1) * HALO
            trail_ref[part, to:, :] = marks
            link_ref[part, past + to :, :] = marks
        down0_ref[half + HALO : half + 2 * HALO, tile:] = marks


def frames_update(amplitude, patches, dual, probe, obj, places, self_index):
    count, modes = dual.shape[:2]
    width = amplitude.shape[-1]
    pairs, perm = dft_weights(width)
    half = width // 2
    tile = obj.shape[1]
    grow = tile + half
    thin = 2 * grow // half * HALO
    last = tile // half - 1
    messages = (
        (2 * modes + 1, half, width),
        (2 * modes + 1, half, width),
        (2, grow, grow),
        (2, grow, half),
        (2, half + 2 * HALO + thin, half),
        (2, thin, half),
        (half + 2 * HALO, grow),
        (half + 2 * HALO, grow),
        (2, 2 * HALO, grow),
    )

    def whole(shape):
        return pl.BlockSpec(shape, lambda f, *_: (0,) * len(shape))

    return pl.pallas_call(
        frames_kernel,
        out_shape=(jax.ShapeDtypeStruct(dual.shape, jnp.float32),)
        + tuple(jax.ShapeDtypeStruct(m, jnp.float32) for m in messages),
        grid_spec=pltpu.PrefetchScalarGridSpec(
            num_scalar_prefetch=2,
            grid=(count,),
            in_specs=[
                pl.BlockSpec((1, width, half), lambda f, *_: (f, 0, 0)),
                pl.BlockSpec((1, width, half), lambda f, *_: (f, 0, 1)),
                pl.BlockSpec((1, 2, width, width), lambda f, *_: (f, 0, 0, 0)),
                pl.BlockSpec((1, modes, 2, width, width), lambda f, *_: (f, 0, 0, 0, 0)),
                whole(probe.shape),
                whole(pairs.shape),
                whole(perm.shape),
                pl.BlockSpec((2, tile, half), lambda f, *_: (0, 0, 0)),
                pl.BlockSpec((2, tile, half), lambda f, *_: (0, 0, last)),
                pl.BlockSpec((2, HALO, tile), lambda f, *_: (0, 0, 0)),
                pl.BlockSpec((2, HALO, tile), lambda f, *_: (0, tile // HALO - 1, 0)),
            ],
            out_specs=[
                pl.BlockSpec((1, modes, 2, width, width), lambda f, *_: (f, 0, 0, 0, 0)),
            ]
            + [whole(m) for m in messages],
            scratch_shapes=[
                pltpu.VMEM((modes, width, width), jnp.float32),
                pltpu.VMEM((modes, width, width), jnp.float32),
                pltpu.VMEM((2 * modes + 1, width, width), jnp.float32),
                pltpu.VMEM((4, 3 * width, width), jnp.bfloat16),
                pltpu.VMEM((4, width, 3 * width), jnp.bfloat16),
            ],
        ),
        compiler_params=pltpu.CompilerParams(vmem_limit_bytes=VMEM_LIMIT),
        cost_estimate=pl.CostEstimate(
            flops=count * modes * 24 * 2 * width**3, bytes_accessed=20 << 20, transcendentals=0
        ),
        name="frames",
    )(
        places, self_index, amplitude, amplitude, patches, dual, probe,
        jnp.asarray(pairs), jnp.asarray(perm), obj, obj, obj, obj,
    )


def weights_kernel(
    self_ref, own_ref, lead_ref, trail_ref, above_ref, below_ref, corner_ref, probe_ref, out_ref,
    sums_ref, marks_ref, sem, *, size, count,
):
    modes = probe_ref.shape[0]
    width = probe_ref.shape[-1]
    half = width // 2
    rows = out_ref.shape[1]
    tile = rows - 2 * HALO
    last = pl.ds(above_ref.shape[0] - HALO, HALO)
    final = pl.ds(tile, half)
    spots = (
        lead_ref.at[0, pl.ds(lead_ref.shape[1] - HALO, HALO), :],
        trail_ref.at[0, pl.ds(trail_ref.shape[1] - HALO, HALO), :],
        above_ref.at[last, final],
        below_ref.at[0, pl.ds(HALO, HALO), final],
        corner_ref.at[0, pl.ds(corner_ref.shape[1] - 2 * HALO, HALO), :],
        corner_ref.at[0, pl.ds(corner_ref.shape[1] - HALO, HALO), :],
        below_ref.at[0, pl.ds(2 * HALO, HALO), pl.ds(tile - half, half)],
        below_ref.at[0, pl.ds(2 * HALO, HALO), final],
    )
    copies = [pltpu.make_async_copy(spot, marks_ref.at[n], sem.at[n]) for n, spot in enumerate(spots)]
    for copy in copies:
        copy.start()
    power = jnp.zeros((width, width), jnp.float32)
    for m in range(modes):
        power += probe_ref[m, 0] * probe_ref[m, 0] + probe_ref[m, 1] * probe_ref[m, 1]
    sums_ref[...] = jnp.zeros_like(sums_ref)

    def place(row, col, present):
        row = row - self_ref[0] * tile
        col = col - self_ref[1] * tile
        reached = (row >= -width) & (row <= tile) & (col >= -width) & (col <= tile)

        @pl.when(present & reached)
        def _():
            at_row = pl.ds(pl.multiple_of(row + width, half), width)
            at_col = pl.ds(pl.multiple_of(col + width, half), width)
            sums_ref[at_row, at_col] += power

    def place_own(frame, carry):
        place(own_ref[frame, 0], own_ref[frame, 1], True)
        return carry

    lax.fori_loop(0, count, place_own, 0)
    for copy in copies:
        copy.wait()

    def place_marked(n, carry):
        source, frame = n // count, n % count
        row = marks_ref[source, 0, frame].astype(jnp.int32)
        col = marks_ref[source, 1, frame].astype(jnp.int32)
        place(row - 1, col - 1, row > 0)
        return carry

    lax.fori_loop(0, len(spots) * count, place_marked, 0)
    low_row, high_row = -self_ref[0] * tile, (size[0] - self_ref[0]) * tile
    low_col, high_col = -self_ref[1] * tile, (size[1] - self_ref[1]) * tile

    chunk = 56

    def finish(step, carry):
        base = pl.multiple_of(step * chunk, 8)
        at = pl.ds(pl.multiple_of(base + width - HALO, 8), chunk)
        den = jnp.concatenate(
            [
                sums_ref[at, width : width + tile],
                edge_block(sums_ref[at, width + tile : width + tile + half], sums_ref[at, half:width]),
            ],
            axis=1,
        )
        row = lax.broadcasted_iota(jnp.int32, den.shape, 0) + (base - HALO)
        lane = lane_of(den.shape)
        col = jnp.where(lane >= tile + half - HALO, lane - (tile + half), lane)
        inside = (row >= low_row) & (row < high_row) & (col >= low_col) & (col < high_col)
        ratio = jnp.where(inside, smooth_weight / (den + (obj_weight + 4.0 * smooth_weight)), 0.0)
        for n in range(out_ref.shape[0]):
            out_ref[n, pl.ds(base, chunk), :] = ratio[:, n * half : (n + 1) * half]
        return carry

    lax.fori_loop(0, rows // chunk, finish, 0)


def object_weights(self_index, positions, messages, probe, tile):
    width = probe.shape[-1]
    half = width // 2
    smem = pl.BlockSpec(memory_space=pltpu.SMEM)
    size = (lax.axis_size("row"), lax.axis_size("col"))
    return pl.pallas_call(
        functools.partial(weights_kernel, size=size, count=positions.shape[0]),
        out_shape=jax.ShapeDtypeStruct((tile // half + 1, tile + 2 * HALO, half), jnp.float32),
        in_specs=[smem] * 2 + [pl.BlockSpec(memory_space=pl.ANY)] * len(messages) + [VMEM_SPEC],
        out_specs=VMEM_SPEC,
        scratch_shapes=[
            pltpu.VMEM((tile + 2 * width, tile + 2 * width), jnp.float32),
            pltpu.SMEM((8, HALO, half), jnp.float32),
            pltpu.SemaphoreType.DMA((8,)),
        ],
        compiler_params=pltpu.CompilerParams(vmem_limit_bytes=20 << 20),
        name="weights",
    )(self_index, positions, *messages, probe)


PAD = 8


def sweeps_kernel(
    canvas_ref, trail_block, obj_ref, lead_block, link_block, below_block, corner_block, above_ref,
    weight_ref, *refs,
):
    field_ref, edge_ref, head_ref, rhs_ref, first_ref, second_ref = refs[-6:]
    trail, lead_ref, link, below_ref, corner_ref = (
        ref.at[0] for ref in (trail_block, lead_block, link_block, below_block, corner_block)
    )
    tile = obj_ref.shape[1]
    half = lead_ref.shape[-1]
    rows = tile + 2 * HALO
    grow = tile + half
    blocks = grow // half
    wide = blocks - 1
    chunk = 56
    tall = half + HALO
    own = slice(PAD + HALO, PAD + HALO + tile)
    upper = slice(PAD, PAD + HALO)
    lower = slice(PAD + HALO + tile, PAD + 2 * HALO + tile)
    near_top = slice(PAD + HALO, PAD + HALO + half)
    lane = lane_of((rows, half))
    corner_below = [below_ref[2 * HALO : 3 * HALO, n * half : (n + 1) * half] for n in range(5)]

    def thin(values, start, count):
        return jnp.concatenate(
            [values[start + n * HALO : start + (n + 1) * HALO, :] for n in range(count)], axis=1
        )

    def halo(middle, above, below):
        return jnp.concatenate(
            [above[:, :half], middle[:, :half] + above[:, half:], middle[:, half:tile], middle[:, tile:] + below],
            axis=1,
        )

    def columns(right_halo, left_halo):
        gap = jnp.zeros((half - 2 * HALO, right_halo.shape[1]), jnp.float32)
        return jnp.concatenate([right_halo, gap, left_halo], axis=0).T[half - HALO : half + tile + HALO]

    nothing = jnp.zeros((HALO, half), jnp.float32)
    sides = columns(
        halo(thin(trail, 0, blocks), thin(corner_ref, tall + 3 * HALO, 2), corner_below[3]),
        halo(thin(link, tall + HALO, blocks), thin(corner_ref, tall, 2), corner_below[1]),
    )
    first_ref[wide, PAD : PAD + rows, :] = columns(
        halo(
            jnp.concatenate([thin(trail, blocks * HALO, blocks - 1), nothing], axis=1),
            jnp.concatenate([thin(corner_ref, tall + 5 * HALO, 1), nothing], axis=1),
            corner_below[4],
        ),
        halo(
            jnp.concatenate([thin(link, tall + HALO + blocks * HALO, blocks - 1), nothing], axis=1),
            jnp.concatenate([thin(corner_ref, tall + 2 * HALO, 1), nothing], axis=1),
            corner_below[2],
        ),
    )
    for n in range(blocks):
        at = slice(n * half, (n + 1) * half)
        if n < wide:
            first_ref[n, upper, :] = above_ref[tall : tall + HALO, at]
            first_ref[n, own, :] = obj_ref[0, :, at]
            first_ref[n, lower, :] = below_ref[HALO : 2 * HALO, at]
        rhs_ref[n, upper, :] = above_ref[:HALO, at]
        rhs_ref[n, own, :] = canvas_ref[0, :tile, at]
        rhs_ref[n, lower, :] = canvas_ref[0, tile : tile + HALO, at] + below_ref[:HALO, at]
        rhs_ref[n, near_top, :] += above_ref[HALO:tall, at]
        for ref in (first_ref, second_ref):
            ref[n, :PAD, :] = jnp.zeros((PAD, half), jnp.float32)
            ref[n, PAD + rows :, :] = jnp.zeros((PAD, half), jnp.float32)
    rhs_ref[0, PAD + HALO : PAD + 2 * HALO + tile, :] += lead_ref[: tile + HALO, :]
    rhs_ref[0, PAD : PAD + tall, :] += corner_ref[:tall, :]
    rhs_ref[0, lower, :] += corner_below[0]
    rhs_ref[wide, PAD : PAD + rows, :] = sides + jnp.where(
        lane < HALO, rhs_ref[wide, PAD : PAD + rows, :], 0.0
    )

    def prepare(step, carry):
        base = pl.multiple_of(step * chunk, 8)
        for n in range(blocks):
            at = pl.ds(base + PAD, chunk)
            rhs_ref[n, at, :] = (rhs_ref[n, at, :] + obj_weight * first_ref[n, at, :]) * (
                weight_ref[n, pl.ds(base, chunk), :] * (1.0 / smooth_weight)
            )
        return carry

    lax.fori_loop(0, rows // chunk, prepare, 0)
    narrow = lane_of((8, half))
    stride = 2 * chunk

    def sweep(source, target):
        def step_rows(step, carry):
            base = pl.multiple_of(step * stride, 8)

            def turned(group):
                at = pl.ds(base + (PAD + 8 * group), 8)
                mids = [source[n, at, :] for n in range(blocks)]
                return [pltpu.roll(m, 1, 1) for m in mids], [pltpu.roll(m, half - 1, 1) for m in mids]

            ahead = turned(0)
            for group in range(stride // 8):
                froms, tos = ahead
                if group + 1 < stride // 8:
                    ahead = turned(group + 1)
                here = base + (PAD + 8 * group)
                for n in range(blocks):
                    west = jnp.where(narrow == 0, froms[n - 1], froms[n])
                    east = jnp.where(narrow == half - 1, tos[(n + 1) % blocks], tos[n])
                    north = source[n, pl.ds(here - 1, 8), :]
                    south = source[n, pl.ds(here + 1, 8), :]
                    target[n, pl.ds(here, 8), :] = rhs_ref[n, pl.ds(here, 8), :] + weight_ref[
                        n, pl.ds(base + 8 * group, 8), :
                    ] * ((north + south) + (west + east))
            return carry

        lax.fori_loop(0, rows // stride, step_rows, 0)

    source, target = first_ref, second_ref
    for _ in range(SWEEPS):
        sweep(source, target)
        source, target = target, source
    for n in range(wide):
        at = slice(n * half, (n + 1) * half)
        field_ref[0, :, at] = source[n, own, :]
        head_ref[:, at] = source[n, near_top, :]
    edge_ref[...] = source[0, own, :]


def object_sweeps(part, canvas, trail, obj, lead, link, below, corner, above, weight, field):
    tile = obj.shape[1]
    half = lead.shape[-1]
    work = pltpu.VMEM((tile // half + 1, tile + 2 * HALO + 2 * PAD, half), jnp.float32)

    def one(shape):
        return pl.BlockSpec((1,) + tuple(shape[1:]), lambda g: (part, 0, 0))

    def whole(shape):
        return pl.BlockSpec(shape, lambda g: (0,) * len(shape))

    blocked = [canvas, trail, obj, lead, link, below, corner]
    extra = [] if field is None else [field]
    return pl.pallas_call(
        sweeps_kernel,
        out_shape=(
            jax.ShapeDtypeStruct(obj.shape, jnp.float32),
            jax.ShapeDtypeStruct((tile, half), jnp.float32),
            jax.ShapeDtypeStruct((half, tile), jnp.float32),
        ),
        grid=(1,),
        in_specs=[one(x.shape) for x in blocked]
        + [whole(above.shape), whole(weight.shape)]
        + [pl.BlockSpec(memory_space=pl.ANY)] * len(extra),
        out_specs=[one(obj.shape), whole((tile, half)), whole((half, tile))],
        scratch_shapes=[work, work, work],
        input_output_aliases={9: 0} if extra else {},
        compiler_params=pltpu.CompilerParams(vmem_limit_bytes=56 << 20),
    )(*blocked, above, weight, *extra)


def corners_kernel(link_block, trail_block, up_ref, corner_ref, below_ref):
    half = link_block.shape[-1]
    grow = up_ref.shape[-1]
    blocks = grow // half
    tall = half + HALO
    first, last = blocks * HALO, (2 * blocks - 2) * HALO
    marks = last + HALO
    past = tall + HALO
    for part in range(2):
        link_ref, trail_ref = link_block.at[part], trail_block.at[part]
        corner_ref[part, :tall, :] = link_ref[:tall, :]
        at = tall
        for ref, base in ((link_ref, past), (trail_ref, 0)):
            corner_ref[part, at : at + 2 * HALO, :] = ref[base + first - 2 * HALO : base + first, :]
            corner_ref[part, at + 2 * HALO : at + 3 * HALO, :] = ref[base + last : base + last + HALO, :]
            at += 3 * HALO
        corner_ref[part, at : at + HALO, :] = link_ref[past + marks : past + marks + HALO, :]
        corner_ref[part, at + HALO : at + 2 * HALO, :] = trail_ref[marks : marks + HALO, :]
        below_ref[part, : 2 * HALO, :] = up_ref[part]
        spots = (
            (link_ref, tall), (link_ref, past), (link_ref, past + first), (trail_ref, 0), (trail_ref, first),
            (link_ref, past + marks), (trail_ref, marks),
        )
        places = [*range(5), blocks - 2, blocks - 1]
        for n, (ref, start) in zip(places, spots):
            below_ref[part, 2 * HALO :, n * half : (n + 1) * half] = ref[start : start + HALO, :]


def corners(link, trail, up):
    grow = up.shape[-1]
    half = link.shape[-1]
    shapes = ((2, half + 9 * HALO, half), (2, 3 * HALO, grow))
    return pl.pallas_call(
        corners_kernel,
        out_shape=tuple(jax.ShapeDtypeStruct(x, jnp.float32) for x in shapes),
        grid=(1,),
        in_specs=[pl.BlockSpec(x.shape, lambda g: (0, 0, 0)) for x in (link, trail, up)],
        out_specs=[pl.BlockSpec(x, lambda g: (0, 0, 0)) for x in shapes],
        compiler_params=pltpu.CompilerParams(vmem_limit_bytes=12 << 20),
        name="corners",
    )(link, trail, up)


def windows_kernel(place_ref, self_ref, field_ref, *refs):
    strips = refs[:-4]
    out_ref, whole_ref, load_sem, store_sem = refs[-4:]
    tile = field_ref.shape[1]
    width = out_ref.shape[-1]
    half = width // 2
    moves = [(field_ref, whole_ref.at[:, :tile, :tile])]
    for part in range(2):
        moves.append((strips[3 * part], whole_ref.at[part, :tile, tile:]))
        moves.append((strips[3 * part + 1], whole_ref.at[part, tile:, tile:]))
        moves.append((strips[3 * part + 2], whole_ref.at[part, tile:, :tile]))
    loads = [
        pltpu.make_async_copy(source, target, load_sem.at[n]) for n, (source, target) in enumerate(moves)
    ]
    for copy in loads:
        copy.start()
    for copy in loads:
        copy.wait()
    stores = []
    for frame in range(out_ref.shape[0]):
        row = pl.multiple_of(place_ref[frame, 0] - self_ref[0] * tile, half)
        col = pl.multiple_of(place_ref[frame, 1] - self_ref[1] * tile, half)
        stores.append(
            pltpu.make_async_copy(
                whole_ref.at[:, pl.ds(row, width), pl.ds(col, width)], out_ref.at[frame], store_sem.at[frame]
            )
        )
    for copy in stores:
        copy.start()
    for copy in stores:
        copy.wait()


def windows(places, self_index, field, strips, width):
    count = places.shape[0]
    grow = field.shape[1] + width // 2
    anywhere = pl.BlockSpec(memory_space=pl.ANY)
    return pl.pallas_call(
        windows_kernel,
        out_shape=jax.ShapeDtypeStruct((count, 2, width, width), jnp.float32),
        in_specs=[pl.BlockSpec(memory_space=pltpu.SMEM)] * 2 + [anywhere] * 7,
        out_specs=anywhere,
        scratch_shapes=[
            pltpu.VMEM((2, grow, grow), jnp.float32),
            pltpu.SemaphoreType.DMA((7,)),
            pltpu.SemaphoreType.DMA((count,)),
        ],
        compiler_params=pltpu.CompilerParams(vmem_limit_bytes=56 << 20),
        name="windows",
    )(places, self_index, field, *strips)


def join_kernel(spot_ref, *refs):
    out_ref = refs[-1]
    rows = refs[0].shape[1]
    for n, ref in enumerate(refs[:-1]):
        at = pl.multiple_of(spot_ref[n] * rows, 8)
        out_ref[:, pl.ds(at, rows), :] = ref[...]


def join(spots, pieces):
    shape = pieces[0].shape
    return pl.pallas_call(
        join_kernel,
        out_shape=jax.ShapeDtypeStruct((shape[0], len(pieces) * shape[1], shape[2]), jnp.float32),
        in_specs=[pl.BlockSpec(memory_space=pltpu.SMEM)] + [VMEM_SPEC] * len(pieces),
        out_specs=VMEM_SPEC,
        compiler_params=pltpu.CompilerParams(vmem_limit_bytes=16 << 20),
        name="join",
    )(spots, *pieces)


def update_probe(keep, give, probe):
    parts = keep.shape[0] - 1
    width = probe.shape[-1]
    rows, cols = lax.axis_size("row"), lax.axis_size("col")
    row_index, col_index = lax.axis_index("row"), lax.axis_index("col")
    core = col_index & 1
    piece = keep + swap(give, 0, 1)
    span = piece.shape[1] // 4
    quarter = (col_index & 2) + (row_index & 1)
    masks = ((0, 2), (1, 0), (1, 2))

    def cut(n):
        return lax.dynamic_slice_in_dim(piece, (quarter ^ n) * span, span, axis=1)

    total = cut(0)
    for row_mask, col_mask in masks:
        n = row_mask + col_mask
        total = total + swap(cut(n), row_mask, col_mask)
    doublings = [(1 << n, 0) for n in range(1, rows.bit_length() - 1)]
    doublings += [(0, 1 << n) for n in range(2, cols.bit_length() - 1)]
    for n, (row_mask, col_mask) in enumerate(doublings):
        total = total + swap(total, row_mask, col_mask)
    offset = core * (width // 2) + quarter * span
    mine = lax.dynamic_slice_in_dim(probe.reshape(parts, width, width), offset, span, axis=1)
    fresh = (total[:parts] + probe_weight * mine) / (total[parts:] + probe_weight)
    pieces = [fresh] + [swap(fresh, r, c) for r, c in masks]
    spots = jnp.stack([quarter] + [quarter ^ (r + c) for r, c in masks]).astype(jnp.int32)
    half = join(spots, pieces)
    other = swap(half, 0, 1)
    return join(jnp.stack([core, 1 - core]).astype(jnp.int32), [half, other]).reshape(probe.shape)


def per_device(amplitude, patches, dual, probe, obj, positions):
    width = amplitude.shape[-1]
    half = width // 2
    tile = obj.shape[1]
    self_index = jnp.stack([lax.axis_index("row"), lax.axis_index("col")]).astype(jnp.int32)

    dual_new, keep, give, canvas, lead, link, trail, down0, down1, up = frames_update(
        amplitude, patches, dual, probe, obj, positions, self_index
    )
    link = shift(link, "col", 1)
    lead = shift(lead, "col", 1)
    trail = shift(trail, "col", -1)
    above0 = shift(down0, "row", 1)
    above1 = shift(down1, "row", 1)
    corner, below = corners(link, trail, up)
    corner = shift(corner, "row", 1)
    below = shift(below, "row", -1)
    weight = object_weights(
        self_index, positions, (link, trail, above0, below, corner), probe, tile
    )
    field, edge0, head0 = object_sweeps(
        0, canvas, trail, obj, lead, link, below, corner, above0, weight, None
    )
    far_below0 = shift(head0, "row", -1)
    field, edge1, head1 = object_sweeps(
        1, canvas, trail, obj, lead, link, below, corner, above1, weight, field
    )
    far_below1 = shift(head1, "row", -1)
    far_right0 = shift(edge0, "col", -1)
    far_right1 = shift(edge1, "col", -1)
    far_corner0 = shift(far_right0[:half, :], "row", -1)
    far_corner1 = shift(far_right1[:half, :], "row", -1)
    probe_new = update_probe(keep, give, probe)
    patches_new = windows(
        positions,
        self_index,
        field,
        (far_right0, far_corner0, far_below0, far_right1, far_corner1, far_below1),
        width,
    )
    return (dual_new, field, probe_new, patches_new)


def solution(mesh):
    return jax.shard_map(
        per_device,
        mesh=mesh,
        in_specs=(
            P(("row", "col"), None, None),
            P(("row", "col"), None, None, None),
            P(("row", "col"), None, None, None, None),
            P(),
            P(None, "row", "col"),
            P(("row", "col"), None),
        ),
        out_specs=(
            P(("row", "col"), None, None, None, None),
            P(None, "row", "col"),
            P(),
            P(("row", "col"), None, None, None),
        ),
        check_vma=False,
    )
```

```python
import functools
import math

import jax
import jax.numpy as jnp
import numpy as np
from jax import lax
from jax.experimental import pallas as pl
from jax.experimental.pallas import tpu as pltpu
from jax.sharding import PartitionSpec as P


SWEEPS = 4
HALO = 8

amp_floor = 1.0
obj_weight = 0.5
smooth_weight = 16.0
probe_weight = 1.0

VMEM_SPEC = pl.BlockSpec(memory_space=pltpu.VMEM)
VMEM_LIMIT = 60 * 1024 * 1024


def shift(block, axis, distance):
    count = lax.axis_size(axis)
    route = [(i, i + distance) for i in range(count) if 0 <= i + distance < count]
    return lax.ppermute(block, axis, route)


def swap(block, row_mask, col_mask):
    rows, cols = lax.axis_size("row"), lax.axis_size("col")
    route = [
        (r * cols + c, (r ^ row_mask) * cols + (c ^ col_mask)) for r in range(rows) for c in range(cols)
    ]
    return lax.ppermute(block, ("row", "col"), route)


def split_two(value):
    high = value.astype(jnp.bfloat16)
    low = (value - high.astype(jnp.float32)).astype(jnp.bfloat16)
    return high, low


def dft_weights(width):
    half = width // 2
    k = np.arange(half)[:, None]
    j = np.arange(half)[None, :]
    mats = []
    for parity in range(2):
        angle = 2.0 * math.pi * ((k * (2 * j + parity)) % width) / width
        re = np.cos(angle) / math.sqrt(width)
        im = -np.sin(angle) / math.sqrt(width)
        mats.append(np.block([[re, im], [-im, re]]))
    pairs = []
    for m in mats + [m.T for m in mats]:
        high = m.astype(np.float32).astype(jnp.bfloat16)
        low = (m - high.astype(np.float64)).astype(np.float32).astype(jnp.bfloat16)
        pairs.append(np.stack([high, low]))
    order = np.concatenate([np.arange(0, width, 2), np.arange(1, width, 2)])
    perm = np.zeros((width, width), np.float32)
    perm[order, np.arange(width)] = 1.0
    return np.stack(pairs), perm.astype(jnp.bfloat16)


def lane_of(shape):
    return lax.broadcasted_iota(jnp.int32, shape, len(shape) - 1)


def edge_block(right_part, left_part):
    lane = lane_of(right_part.shape)
    width = right_part.shape[-1]
    return jnp.where(lane < HALO, right_part, jnp.where(lane >= width - HALO, left_part, 0.0))


def frames_kernel(
    place_ref, self_ref, amp_low_ref, amp_high_ref, patch_ref, dual_ref, probe_ref, pair_ref, perm_ref,
    obj_low_ref, obj_high_ref, obj_first_ref, obj_last_ref,
    new_ref, keep_ref, give_ref, canvas_ref, lead_ref, link_ref, trail_ref, down0_ref, down1_ref, up_ref,
    even_ref, odd_ref, num_ref, right_ref, left_ref,
):
    frame = pl.program_id(0)
    modes = probe_ref.shape[0]
    width = probe_ref.shape[-1]
    half = width // 2

    @pl.when(frame == 0)
    def _():
        canvas_ref[...] = jnp.zeros_like(canvas_ref)
        num_ref[...] = jnp.zeros_like(num_ref)
        for n in range(4):
            high, low = pair_ref[n, 0], pair_ref[n, 1]
            for k, m in enumerate((high, high, low)):
                right_ref[n, k * width : (k + 1) * width, :] = m
            for k, m in enumerate((high, low, high)):
                left_ref[(n + 2) % 4, :, k * width : (k + 1) * width] = m

    def dot(a, b):
        return jnp.dot(a, b, preferred_element_type=jnp.float32)

    def times_right(value, which):
        high, low = split_two(value)
        return dot(jnp.concatenate([high, low, high], axis=1), right_ref[which])

    def times_left(which, value):
        high, low = split_two(value)
        return dot(left_ref[which], jnp.concatenate([high, high, low], axis=0))

    patch_re = patch_ref[0, 0]
    patch_im = patch_ref[0, 1]

    def exit_wave(m):
        probe_re = probe_ref[m, 0]
        probe_im = probe_ref[m, 1]
        return probe_re * patch_re - probe_im * patch_im, probe_re * patch_im + probe_im * patch_re

    amps = []
    for parity in range(2):
        every = pl.ds(parity, half, stride=2)
        rows = jnp.concatenate([amp_low_ref[0, every, :], amp_high_ref[0, every, :]], axis=1)
        first = rows.astype(jnp.bfloat16)
        rest = rows - first.astype(jnp.float32)
        second, third = split_two(rest)
        amps.append(dot(first, perm_ref[...]) + (dot(second, perm_ref[...]) + dot(third, perm_ref[...])))

    power = [None, None]
    for m in range(modes):
        exit_re, exit_im = exit_wave(m)
        wave_re = exit_re + dual_ref[0, m, 0]
        wave_im = exit_im + dual_ref[0, m, 1]
        sums = jnp.concatenate(
            [wave_re[:, :half] + wave_re[:, half:], wave_im[:, :half] + wave_im[:, half:]], axis=1
        )
        diffs = jnp.concatenate(
            [wave_re[:, :half] - wave_re[:, half:], wave_im[:, :half] - wave_im[:, half:]], axis=1
        )
        even = times_right(sums, 0)
        odd = times_right(diffs, 1)

        def stack(op):
            return jnp.concatenate(
                [
                    jnp.concatenate([op(x[:half, part], x[half:, part]) for x in (even, odd)], axis=1)
                    for part in (slice(0, half), slice(half, width))
                ],
                axis=0,
            )

        even_ref[m] = stack(lambda a, b: a + b)
        odd_ref[m] = stack(lambda a, b: a - b)

    for m in range(modes):
        far_even = times_left(0, even_ref[m])
        far_odd = times_left(1, odd_ref[m])
        even_ref[m] = far_even
        odd_ref[m] = far_odd
        for parity, far in enumerate((far_even, far_odd)):
            term = far[:half] * far[:half] + far[half:] * far[half:]
            power[parity] = term if m == 0 else power[parity] + term

    ratios = []
    for parity in range(2):
        ratio = amps[parity] / jnp.sqrt(power[parity] + amp_floor)
        ratios.append(jnp.concatenate([ratio, ratio], axis=0))

    tile = canvas_ref.shape[1] - half
    start_row = pl.multiple_of(place_ref[frame, 0] - self_ref[0] * tile, half)
    start_col = pl.multiple_of(place_ref[frame, 1] - self_ref[1] * tile, half)
    obj_re = jnp.zeros((width, width), jnp.float32)
    obj_im = jnp.zeros((width, width), jnp.float32)
    for m in range(modes):
        even = times_left(2, even_ref[m] * ratios[0])
        odd = times_left(3, odd_ref[m] * ratios[1])
        top = even + odd
        bottom = even - odd

        def rows_of(part):
            return jnp.concatenate(
                [
                    jnp.concatenate([x[:half, part], x[half:, part]], axis=1)
                    for x in (top, bottom)
                ],
                axis=0,
            )

        even_ref[m] = rows_of(slice(0, half))
        odd_ref[m] = rows_of(slice(half, width))

    for m in range(modes):
        even = times_right(even_ref[m], 2)
        odd = times_right(odd_ref[m], 3)
        low = even + odd
        high = even - odd
        near_re = jnp.concatenate([low[:, :half], high[:, :half]], axis=1)
        near_im = jnp.concatenate([low[:, half:], high[:, half:]], axis=1)
        exit_re, exit_im = exit_wave(m)
        new_re = dual_ref[0, m, 0] + exit_re - near_re
        new_im = dual_ref[0, m, 1] + exit_im - near_im
        new_ref[0, m, 0] = new_re
        new_ref[0, m, 1] = new_im
        target_re = near_re - new_re
        target_im = near_im - new_im
        num_ref[2 * m] += patch_re * target_re + patch_im * target_im
        num_ref[2 * m + 1] += patch_re * target_im - patch_im * target_re
        probe_re = probe_ref[m, 0]
        probe_im = probe_ref[m, 1]
        obj_re += probe_re * target_re + probe_im * target_im
        obj_im += probe_re * target_im - probe_im * target_re
    num_ref[2 * modes] += patch_re * patch_re + patch_im * patch_im
    canvas_ref[0, pl.ds(start_row, width), pl.ds(start_col, width)] += obj_re
    canvas_ref[1, pl.ds(start_row, width), pl.ds(start_col, width)] += obj_im

    @pl.when(frame == pl.num_programs(0) - 1)
    def _():
        grow = canvas_ref.shape[1]
        blocks = grow // half
        kept = pl.multiple_of((self_ref[1] & 1) * half, half)
        given = pl.multiple_of((1 - (self_ref[1] & 1)) * half, half)
        keep_ref[...] = num_ref[:, pl.ds(kept, half), :]
        give_ref[...] = num_ref[:, pl.ds(given, half), :]
        shape = (HALO, half)
        lane = lane_of(shape)
        row = lax.broadcasted_iota(jnp.int32, shape, 0)
        marks = jnp.zeros(shape, jnp.int32)
        for n in range(place_ref.shape[0]):
            for part in range(2):
                marks = jnp.where((lane == n) & (row == part), place_ref[n, part] + 1, marks)
        marks = marks.astype(jnp.float32)
        for part, down_ref in enumerate((down0_ref, down1_ref)):
            down_ref[: half + HALO, :] = canvas_ref[part, tile - HALO :, :]
            down_ref[half + HALO : half + 2 * HALO, :tile] = obj_last_ref[part]
            down_ref[half + HALO : half + 2 * HALO, tile:] = jnp.zeros(shape, jnp.float32)
            lead_ref[part] = canvas_ref[part, :, tile:]
            link_ref[part, : half + HALO, :] = canvas_ref[part, tile - HALO :, tile:]
            link_ref[part, half + HALO : half + 2 * HALO, :] = canvas_ref[part, :HALO, tile:]
            past = half + 2 * HALO
            up_ref[part, :HALO, :] = canvas_ref[part, :HALO, :]
            up_ref[part, HALO:, :tile] = obj_first_ref[part]
            up_ref[part, HALO:, tile:] = marks
            sums = edge_block(canvas_ref[part, :, :half], canvas_ref[part, :, tile - half : tile]).T
            objs = edge_block(obj_low_ref[part], obj_high_ref[part]).T
            for ends, count, base in ((sums, blocks, 0), (objs, blocks - 1, blocks)):
                for n in range(count):
                    at = slice(n * half, (n + 1) * half)
                    to = (base + n) * HALO
                    trail_ref[part, to : to + HALO, :] = ends[:HALO, at]
                    link_ref[part, past + to : past + to + HALO, :] = ends[half - HALO :, at]
            to = (2 * blocks - 1) * HALO
            trail_ref[part, to:, :] = marks
            link_ref[part, past + to :, :] = marks
        down0_ref[half + HALO : half + 2 * HALO, tile:] = marks


def frames_update(amplitude, patches, dual, probe, obj, places, self_index):
    count, modes = dual.shape[:2]
    width = amplitude.shape[-1]
    pairs, perm = dft_weights(width)
    half = width // 2
    tile = obj.shape[1]
    grow = tile + half
    thin = 2 * grow // half * HALO
    last = tile // half - 1
    messages = (
        (2 * modes + 1, half, width),
        (2 * modes + 1, half, width),
        (2, grow, grow),
        (2, grow, half),
        (2, half + 2 * HALO + thin, half),
        (2, thin, half),
        (half + 2 * HALO, grow),
        (half + 2 * HALO, grow),
        (2, 2 * HALO, grow),
    )

    def whole(shape):
        return pl.BlockSpec(shape, lambda f, *_: (0,) * len(shape))

    return pl.pallas_call(
        frames_kernel,
        out_shape=(jax.ShapeDtypeStruct(dual.shape, jnp.float32),)
        + tuple(jax.ShapeDtypeStruct(m, jnp.float32) for m in messages),
        grid_spec=pltpu.PrefetchScalarGridSpec(
            num_scalar_prefetch=2,
            grid=(count,),
            in_specs=[
                pl.BlockSpec((1, width, half), lambda f, *_: (f, 0, 0)),
                pl.BlockSpec((1, width, half), lambda f, *_: (f, 0, 1)),
                pl.BlockSpec((1, 2, width, width), lambda f, *_: (f, 0, 0, 0)),
                pl.BlockSpec((1, modes, 2, width, width), lambda f, *_: (f, 0, 0, 0, 0)),
                whole(probe.shape),
                whole(pairs.shape),
                whole(perm.shape),
                pl.BlockSpec((2, tile, half), lambda f, *_: (0, 0, 0)),
                pl.BlockSpec((2, tile, half), lambda f, *_: (0, 0, last)),
                pl.BlockSpec((2, HALO, tile), lambda f, *_: (0, 0, 0)),
                pl.BlockSpec((2, HALO, tile), lambda f, *_: (0, tile // HALO - 1, 0)),
            ],
            out_specs=[
                pl.BlockSpec((1, modes, 2, width, width), lambda f, *_: (f, 0, 0, 0, 0)),
            ]
            + [whole(m) for m in messages],
            scratch_shapes=[
                pltpu.VMEM((modes, width, width), jnp.float32),
                pltpu.VMEM((modes, width, width), jnp.float32),
                pltpu.VMEM((2 * modes + 1, width, width), jnp.float32),
                pltpu.VMEM((4, 3 * width, width), jnp.bfloat16),
                pltpu.VMEM((4, width, 3 * width), jnp.bfloat16),
            ],
        ),
        compiler_params=pltpu.CompilerParams(vmem_limit_bytes=VMEM_LIMIT),
        cost_estimate=pl.CostEstimate(
            flops=count * modes * 24 * 2 * width**3, bytes_accessed=20 << 20, transcendentals=0
        ),
        name="frames",
    )(
        places, self_index, amplitude, amplitude, patches, dual, probe,
        jnp.asarray(pairs), jnp.asarray(perm), obj, obj, obj, obj,
    )


def weights_kernel(
    self_ref, own_ref, lead_ref, trail_ref, above_ref, below_ref, corner_ref, probe_ref, out_ref,
    sums_ref, marks_ref, sem, *, size, count,
):
    modes = probe_ref.shape[0]
    width = probe_ref.shape[-1]
    half = width // 2
    rows = out_ref.shape[1]
    tile = rows - 2 * HALO
    last = pl.ds(above_ref.shape[0] - HALO, HALO)
    final = pl.ds(tile, half)
    spots = (
        lead_ref.at[0, pl.ds(lead_ref.shape[1] - HALO, HALO), :],
        trail_ref.at[0, pl.ds(trail_ref.shape[1] - HALO, HALO), :],
        above_ref.at[last, final],
        below_ref.at[0, pl.ds(HALO, HALO), final],
        corner_ref.at[0, pl.ds(corner_ref.shape[1] - 2 * HALO, HALO), :],
        corner_ref.at[0, pl.ds(corner_ref.shape[1] - HALO, HALO), :],
        below_ref.at[0, pl.ds(2 * HALO, HALO), pl.ds(tile - half, half)],
        below_ref.at[0, pl.ds(2 * HALO, HALO), final],
    )
    copies = [pltpu.make_async_copy(spot, marks_ref.at[n], sem.at[n]) for n, spot in enumerate(spots)]
    for copy in copies:
        copy.start()
    power = jnp.zeros((width, width), jnp.float32)
    for m in range(modes):
        power += probe_ref[m, 0] * probe_ref[m, 0] + probe_ref[m, 1] * probe_ref[m, 1]
    sums_ref[...] = jnp.zeros_like(sums_ref)

    def place(row, col, present):
        row = row - self_ref[0] * tile
        col = col - self_ref[1] * tile
        reached = (row >= -width) & (row <= tile) & (col >= -width) & (col <= tile)

        @pl.when(present & reached)
        def _():
            at_row = pl.ds(pl.multiple_of(row + width, half), width)
            at_col = pl.ds(pl.multiple_of(col + width, half), width)
            sums_ref[at_row, at_col] += power

    def place_own(frame, carry):
        place(own_ref[frame, 0], own_ref[frame, 1], True)
        return carry

    lax.fori_loop(0, count, place_own, 0)
    for copy in copies:
        copy.wait()

    def place_marked(n, carry):
        source, frame = n // count, n % count
        row = marks_ref[source, 0, frame].astype(jnp.int32)
        col = marks_ref[source, 1, frame].astype(jnp.int32)
        place(row - 1, col - 1, row > 0)
        return carry

    lax.fori_loop(0, len(spots) * count, place_marked, 0)
    low_row, high_row = -self_ref[0] * tile, (size[0] - self_ref[0]) * tile
    low_col, high_col = -self_ref[1] * tile, (size[1] - self_ref[1]) * tile

    chunk = 56

    def finish(step, carry):
        base = pl.multiple_of(step * chunk, 8)
        at = pl.ds(pl.multiple_of(base + width - HALO, 8), chunk)
        den = jnp.concatenate(
            [
                sums_ref[at, width : width + tile],
                edge_block(sums_ref[at, width + tile : width + tile + half], sums_ref[at, half:width]),
            ],
            axis=1,
        )
        row = lax.broadcasted_iota(jnp.int32, den.shape, 0) + (base - HALO)
        lane = lane_of(den.shape)
        col = jnp.where(lane >= tile + half - HALO, lane - (tile + half), lane)
        inside = (row >= low_row) & (row < high_row) & (col >= low_col) & (col < high_col)
        ratio = jnp.where(inside, smooth_weight / (den + (obj_weight + 4.0 * smooth_weight)), 0.0)
        for n in range(out_ref.shape[0]):
            out_ref[n, pl.ds(base, chunk), :] = ratio[:, n * half : (n + 1) * half]
        return carry

    lax.fori_loop(0, rows // chunk, finish, 0)


def object_weights(self_index, positions, messages, probe, tile):
    width = probe.shape[-1]
    half = width // 2
    smem = pl.BlockSpec(memory_space=pltpu.SMEM)
    size = (lax.axis_size("row"), lax.axis_size("col"))
    return pl.pallas_call(
        functools.partial(weights_kernel, size=size, count=positions.shape[0]),
        out_shape=jax.ShapeDtypeStruct((tile // half + 1, tile + 2 * HALO, half), jnp.float32),
        in_specs=[smem] * 2 + [pl.BlockSpec(memory_space=pl.ANY)] * len(messages) + [VMEM_SPEC],
        out_specs=VMEM_SPEC,
        scratch_shapes=[
            pltpu.VMEM((tile + 2 * width, tile + 2 * width), jnp.float32),
            pltpu.SMEM((8, HALO, half), jnp.float32),
            pltpu.SemaphoreType.DMA((8,)),
        ],
        compiler_params=pltpu.CompilerParams(vmem_limit_bytes=20 << 20),
        name="weights",
    )(self_index, positions, *messages, probe)


PAD = 8


def sweeps_kernel(
    canvas_ref, trail_block, obj_ref, lead_block, link_block, below_block, corner_block, above_ref,
    weight_ref, *refs,
):
    field_ref, edge_ref, head_ref, rhs_ref, first_ref, second_ref = refs[-6:]
    trail, lead_ref, link, below_ref, corner_ref = (
        ref.at[0] for ref in (trail_block, lead_block, link_block, below_block, corner_block)
    )
    tile = obj_ref.shape[1]
    half = lead_ref.shape[-1]
    rows = tile + 2 * HALO
    grow = tile + half
    blocks = grow // half
    wide = blocks - 1
    chunk = 56
    tall = half + HALO
    own = slice(PAD + HALO, PAD + HALO + tile)
    upper = slice(PAD, PAD + HALO)
    lower = slice(PAD + HALO + tile, PAD + 2 * HALO + tile)
    near_top = slice(PAD + HALO, PAD + HALO + half)
    lane = lane_of((rows, half))
    corner_below = [below_ref[2 * HALO : 3 * HALO, n * half : (n + 1) * half] for n in range(5)]

    def thin(values, start, count):
        return jnp.concatenate(
            [values[start + n * HALO : start + (n + 1) * HALO, :] for n in range(count)], axis=1
        )

    def halo(middle, above, below):
        return jnp.concatenate(
            [above[:, :half], middle[:, :half] + above[:, half:], middle[:, half:tile], middle[:, tile:] + below],
            axis=1,
        )

    def columns(right_halo, left_halo):
        gap = jnp.zeros((half - 2 * HALO, right_halo.shape[1]), jnp.float32)
        return jnp.concatenate([right_halo, gap, left_halo], axis=0).T[half - HALO : half + tile + HALO]

    nothing = jnp.zeros((HALO, half), jnp.float32)
    sides = columns(
        halo(thin(trail, 0, blocks), thin(corner_ref, tall + 3 * HALO, 2), corner_below[3]),
        halo(thin(link, tall + HALO, blocks), thin(corner_ref, tall, 2), corner_below[1]),
    )
    first_ref[wide, PAD : PAD + rows, :] = columns(
        halo(
            jnp.concatenate([thin(trail, blocks * HALO, blocks - 1), nothing], axis=1),
            jnp.concatenate([thin(corner_ref, tall + 5 * HALO, 1), nothing], axis=1),
            corner_below[4],
        ),
        halo(
            jnp.concatenate([thin(link, tall + HALO + blocks * HALO, blocks - 1), nothing], axis=1),
            jnp.concatenate([thin(corner_ref, tall + 2 * HALO, 1), nothing], axis=1),
            corner_below[2],
        ),
    )
    for n in range(blocks):
        at = slice(n * half, (n + 1) * half)
        if n < wide:
            first_ref[n, upper, :] = above_ref[tall : tall + HALO, at]
            first_ref[n, own, :] = obj_ref[0, :, at]
            first_ref[n, lower, :] = below_ref[HALO : 2 * HALO, at]
        rhs_ref[n, upper, :] = above_ref[:HALO, at]
        rhs_ref[n, own, :] = canvas_ref[0, :tile, at]
        rhs_ref[n, lower, :] = canvas_ref[0, tile : tile + HALO, at] + below_ref[:HALO, at]
        rhs_ref[n, near_top, :] += above_ref[HALO:tall, at]
        for ref in (first_ref, second_ref):
            ref[n, :PAD, :] = jnp.zeros((PAD, half), jnp.float32)
            ref[n, PAD + rows :, :] = jnp.zeros((PAD, half), jnp.float32)
    rhs_ref[0, PAD + HALO : PAD + 2 * HALO + tile, :] += lead_ref[: tile + HALO, :]
    rhs_ref[0, PAD : PAD + tall, :] += corner_ref[:tall, :]
    rhs_ref[0, lower, :] += corner_below[0]
    rhs_ref[wide, PAD : PAD + rows, :] = sides + jnp.where(
        lane < HALO, rhs_ref[wide, PAD : PAD + rows, :], 0.0
    )

    def prepare(step, carry):
        base = pl.multiple_of(step * chunk, 8)
        for n in range(blocks):
            at = pl.ds(base + PAD, chunk)
            rhs_ref[n, at, :] = (rhs_ref[n, at, :] + obj_weight * first_ref[n, at, :]) * (
                weight_ref[n, pl.ds(base, chunk), :] * (1.0 / smooth_weight)
            )
        return carry

    lax.fori_loop(0, rows // chunk, prepare, 0)
    narrow = lane_of((8, half))
    stride = 2 * chunk

    def sweep(source, target):
        def step_rows(step, carry):
            base = pl.multiple_of(step * stride, 8)

            def turned(group):
                at = pl.ds(base + (PAD + 8 * group), 8)
                mids = [source[n, at, :] for n in range(blocks)]
                return [pltpu.roll(m, 1, 1) for m in mids], [pltpu.roll(m, half - 1, 1) for m in mids]

            ahead = turned(0)
            for group in range(stride // 8):
                froms, tos = ahead
                if group + 1 < stride // 8:
                    ahead = turned(group + 1)
                here = base + (PAD + 8 * group)
                for n in range(blocks):
                    west = jnp.where(narrow == 0, froms[n - 1], froms[n])
                    east = jnp.where(narrow == half - 1, tos[(n + 1) % blocks], tos[n])
                    north = source[n, pl.ds(here - 1, 8), :]
                    south = source[n, pl.ds(here + 1, 8), :]
                    target[n, pl.ds(here, 8), :] = rhs_ref[n, pl.ds(here, 8), :] + weight_ref[
                        n, pl.ds(base + 8 * group, 8), :
                    ] * ((north + south) + (west + east))
            return carry

        lax.fori_loop(0, rows // stride, step_rows, 0)

    source, target = first_ref, second_ref
    for _ in range(SWEEPS):
        sweep(source, target)
        source, target = target, source
    for n in range(wide):
        at = slice(n * half, (n + 1) * half)
        field_ref[0, :, at] = source[n, own, :]
        head_ref[:, at] = source[n, near_top, :]
    edge_ref[...] = source[0, own, :]


def object_sweeps(part, canvas, trail, obj, lead, link, below, corner, above, weight, field):
    tile = obj.shape[1]
    half = lead.shape[-1]
    work = pltpu.VMEM((tile // half + 1, tile + 2 * HALO + 2 * PAD, half), jnp.float32)

    def one(shape):
        return pl.BlockSpec((1,) + tuple(shape[1:]), lambda g: (part, 0, 0))

    def whole(shape):
        return pl.BlockSpec(shape, lambda g: (0,) * len(shape))

    blocked = [canvas, trail, obj, lead, link, below, corner]
    extra = [] if field is None else [field]
    return pl.pallas_call(
        sweeps_kernel,
        out_shape=(
            jax.ShapeDtypeStruct(obj.shape, jnp.float32),
            jax.ShapeDtypeStruct((tile, half), jnp.float32),
            jax.ShapeDtypeStruct((half, tile), jnp.float32),
        ),
        grid=(1,),
        in_specs=[one(x.shape) for x in blocked]
        + [whole(above.shape), whole(weight.shape)]
        + [pl.BlockSpec(memory_space=pl.ANY)] * len(extra),
        out_specs=[one(obj.shape), whole((tile, half)), whole((half, tile))],
        scratch_shapes=[work, work, work],
        input_output_aliases={9: 0} if extra else {},
        compiler_params=pltpu.CompilerParams(vmem_limit_bytes=56 << 20),
    )(*blocked, above, weight, *extra)


def corners_kernel(link_block, trail_block, up_ref, corner_ref, below_ref):
    half = link_block.shape[-1]
    grow = up_ref.shape[-1]
    blocks = grow // half
    tall = half + HALO
    first, last = blocks * HALO, (2 * blocks - 2) * HALO
    marks = last + HALO
    past = tall + HALO
    for part in range(2):
        link_ref, trail_ref = link_block.at[part], trail_block.at[part]
        corner_ref[part, :tall, :] = link_ref[:tall, :]
        at = tall
        for ref, base in ((link_ref, past), (trail_ref, 0)):
            corner_ref[part, at : at + 2 * HALO, :] = ref[base + first - 2 * HALO : base + first, :]
            corner_ref[part, at + 2 * HALO : at + 3 * HALO, :] = ref[base + last : base + last + HALO, :]
            at += 3 * HALO
        corner_ref[part, at : at + HALO, :] = link_ref[past + marks : past + marks + HALO, :]
        corner_ref[part, at + HALO : at + 2 * HALO, :] = trail_ref[marks : marks + HALO, :]
        below_ref[part, : 2 * HALO, :] = up_ref[part]
        spots = (
            (link_ref, tall), (link_ref, past), (link_ref, past + first), (trail_ref, 0), (trail_ref, first),
            (link_ref, past + marks), (trail_ref, marks),
        )
        places = [*range(5), blocks - 2, blocks - 1]
        for n, (ref, start) in zip(places, spots):
            below_ref[part, 2 * HALO :, n * half : (n + 1) * half] = ref[start : start + HALO, :]


def corners(link, trail, up):
    grow = up.shape[-1]
    half = link.shape[-1]
    shapes = ((2, half + 9 * HALO, half), (2, 3 * HALO, grow))
    return pl.pallas_call(
        corners_kernel,
        out_shape=tuple(jax.ShapeDtypeStruct(x, jnp.float32) for x in shapes),
        grid=(1,),
        in_specs=[pl.BlockSpec(x.shape, lambda g: (0, 0, 0)) for x in (link, trail, up)],
        out_specs=[pl.BlockSpec(x, lambda g: (0, 0, 0)) for x in shapes],
        compiler_params=pltpu.CompilerParams(vmem_limit_bytes=12 << 20),
        name="corners",
    )(link, trail, up)


def windows_kernel(place_ref, self_ref, field_ref, *refs):
    strips = refs[:-4]
    out_ref, block_ref, load_sem, store_sem = refs[-4:]
    tile = field_ref.shape[1]
    width = out_ref.shape[-1]
    half = width // 2
    quadrants = [(down, right) for down in range(2) for right in range(2)]

    def spot(frame, part, down, right):
        return block_ref.at[
            frame, part, down * half : (down + 1) * half, right * half : (right + 1) * half
        ]

    for frame in range(out_ref.shape[0]):
        for n, (down, right) in enumerate(quadrants):
            row = pl.multiple_of(place_ref[frame, 0] - self_ref[0] * tile + down * half, half)
            col = pl.multiple_of(place_ref[frame, 1] - self_ref[1] * tile + right * half, half)
            above, before = row < tile, col < tile
            for part in range(2):
                side_ref, corner_ref, below_ref = strips[3 * part : 3 * part + 3]
                sem = load_sem.at[frame, n, part]

                def fetch(source):
                    pltpu.make_async_copy(source, spot(frame, part, down, right), sem).start()

                @pl.when(above & before)
                def _():
                    fetch(field_ref.at[part, pl.ds(row, half), pl.ds(col, half)])

                @pl.when(above & jnp.logical_not(before))
                def _():
                    fetch(side_ref.at[pl.ds(row, half), :])

                @pl.when(jnp.logical_not(above) & before)
                def _():
                    fetch(below_ref.at[:, pl.ds(col, half)])

                @pl.when(jnp.logical_not(above | before))
                def _():
                    fetch(corner_ref)

    stores = []
    for frame in range(out_ref.shape[0]):
        for n, (down, right) in enumerate(quadrants):
            for part in range(2):
                pltpu.make_async_copy(
                    strips[1], spot(frame, part, down, right), load_sem.at[frame, n, part]
                ).wait()
        stores.append(pltpu.make_async_copy(block_ref.at[frame], out_ref.at[frame], store_sem.at[frame]))
        stores[-1].start()
    for copy in stores:
        copy.wait()


def windows(places, self_index, field, strips, width):
    count = places.shape[0]
    anywhere = pl.BlockSpec(memory_space=pl.ANY)
    return pl.pallas_call(
        windows_kernel,
        out_shape=jax.ShapeDtypeStruct((count, 2, width, width), jnp.float32),
        in_specs=[pl.BlockSpec(memory_space=pltpu.SMEM)] * 2 + [anywhere] * 7,
        out_specs=anywhere,
        scratch_shapes=[
            pltpu.VMEM((count, 2, width, width), jnp.float32),
            pltpu.SemaphoreType.DMA((count, 4, 2)),
            pltpu.SemaphoreType.DMA((count,)),
        ],
        compiler_params=pltpu.CompilerParams(vmem_limit_bytes=56 << 20),
        name="windows",
    )(places, self_index, field, *strips)


def join_kernel(spot_ref, *refs):
    out_ref = refs[-1]
    rows = refs[0].shape[1]
    for n, ref in enumerate(refs[:-1]):
        at = pl.multiple_of(spot_ref[n] * rows, 8)
        out_ref[:, pl.ds(at, rows), :] = ref[...]


def join(spots, pieces):
    shape = pieces[0].shape
    return pl.pallas_call(
        join_kernel,
        out_shape=jax.ShapeDtypeStruct((shape[0], len(pieces) * shape[1], shape[2]), jnp.float32),
        in_specs=[pl.BlockSpec(memory_space=pltpu.SMEM)] + [VMEM_SPEC] * len(pieces),
        out_specs=VMEM_SPEC,
        compiler_params=pltpu.CompilerParams(vmem_limit_bytes=16 << 20),
        name="join",
    )(spots, *pieces)


def update_probe(keep, give, probe):
    parts = keep.shape[0] - 1
    width = probe.shape[-1]
    rows, cols = lax.axis_size("row"), lax.axis_size("col")
    row_index, col_index = lax.axis_index("row"), lax.axis_index("col")
    core = col_index & 1
    piece = keep + swap(give, 0, 1)
    span = piece.shape[1] // 4
    quarter = (col_index & 2) + (row_index & 1)
    masks = ((0, 2), (1, 0), (1, 2))

    def cut(n):
        return lax.dynamic_slice_in_dim(piece, (quarter ^ n) * span, span, axis=1)

    total = cut(0)
    for row_mask, col_mask in masks:
        n = row_mask + col_mask
        total = total + swap(cut(n), row_mask, col_mask)
    doublings = [(1 << n, 0) for n in range(1, rows.bit_length() - 1)]
    doublings += [(0, 1 << n) for n in range(2, cols.bit_length() - 1)]
    for n, (row_mask, col_mask) in enumerate(doublings):
        total = total + swap(total, row_mask, col_mask)
    offset = core * (width // 2) + quarter * span
    mine = lax.dynamic_slice_in_dim(probe.reshape(parts, width, width), offset, span, axis=1)
    fresh = (total[:parts] + probe_weight * mine) / (total[parts:] + probe_weight)
    pieces = [fresh] + [swap(fresh, r, c) for r, c in masks]
    spots = jnp.stack([quarter] + [quarter ^ (r + c) for r, c in masks]).astype(jnp.int32)
    half = join(spots, pieces)
    other = swap(half, 0, 1)
    return join(jnp.stack([core, 1 - core]).astype(jnp.int32), [half, other]).reshape(probe.shape)


def per_device(amplitude, patches, dual, probe, obj, positions):
    width = amplitude.shape[-1]
    half = width // 2
    tile = obj.shape[1]
    self_index = jnp.stack([lax.axis_index("row"), lax.axis_index("col")]).astype(jnp.int32)

    dual_new, keep, give, canvas, lead, link, trail, down0, down1, up = frames_update(
        amplitude, patches, dual, probe, obj, positions, self_index
    )
    link = shift(link, "col", 1)
    lead = shift(lead, "col", 1)
    trail = shift(trail, "col", -1)
    above0 = shift(down0, "row", 1)
    above1 = shift(down1, "row", 1)
    corner, below = corners(link, trail, up)
    corner = shift(corner, "row", 1)
    below = shift(below, "row", -1)
    weight = object_weights(
        self_index, positions, (link, trail, above0, below, corner), probe, tile
    )
    field, edge0, head0 = object_sweeps(
        0, canvas, trail, obj, lead, link, below, corner, above0, weight, None
    )
    far_below0 = shift(head0, "row", -1)
    field, edge1, head1 = object_sweeps(
        1, canvas, trail, obj, lead, link, below, corner, above1, weight, field
    )
    far_below1 = shift(head1, "row", -1)
    far_right0 = shift(edge0, "col", -1)
    far_right1 = shift(edge1, "col", -1)
    far_corner0 = shift(far_right0[:half, :], "row", -1)
    far_corner1 = shift(far_right1[:half, :], "row", -1)
    probe_new = update_probe(keep, give, probe)
    patches_new = windows(
        positions,
        self_index,
        field,
        (far_right0, far_corner0, far_below0, far_right1, far_corner1, far_below1),
        width,
    )
    return (dual_new, field, probe_new, patches_new)


def solution(mesh):
    return jax.shard_map(
        per_device,
        mesh=mesh,
        in_specs=(
            P(("row", "col"), None, None),
            P(("row", "col"), None, None, None),
            P(("row", "col"), None, None, None, None),
            P(),
            P(None, "row", "col"),
            P(("row", "col"), None),
        ),
        out_specs=(
            P(("row", "col"), None, None, None, None),
            P(None, "row", "col"),
            P(),
            P(("row", "col"), None, None, None),
        ),
        check_vma=False,
    )
```
